32 devices in a mesh: member: 2 (over y), lat: 4 (over z), lev: 2 (over x), lon: 2 (over core).
Axes of the slice: x: 2, y: 2, z: 4, core: 2. Of those that a mesh axis runs over, the one named last changes fastest.
Arguments:
- land_mask: int32 [72, 128, 768], P('lev', 'lat', 'lon'), may hold values 0 or 1
- diffusivity: float32 [72, 128, 768], P('lev', 'lat', 'lon'), may hold values from 0.3 to 3
- balance: float32 [72, 72], replicated, may hold values from -0.75 to 0.75
- member_id: int32 [2], P('member'), parts along dimension 0, may hold values from 0 to 63
- counter_key: int32 [2], P('member'), parts along dimension 0, may hold values from 0 to 1048575
Outputs:
- perturbation: float32 [144, 128, 768], P('member', ('lat', 'lev'), 'lon'), parts along dimension 0
The draws below stay inside these ranges and needn't reach their ends.
There are 2 independent parts, one for each index of `member`. The reference program is written for one: setup_inputs(seed, part) draws one part's arguments, and reference() takes and returns one part's arrays. A program takes and returns all parts, laid end to end along the dimension named above; an argument that names none is the same for every part. Nothing has to cross between parts.
All inputs are finite; a program needn't handle non-finite values. No bound on the sum of `land_mask` on one device may be relied on, other than what follows from the above.
Results may differ from the reference program's by a relative error of at most 0.00009.
Values sent between devices are 32-bit elements; how exact they have to be, the bound alone decides.
No kernel may reach another device: no remote copies, remote signals or barrier semaphores. Data moves between devices by JAX's collectives and lax.ppermute only.
A program may use at most 192 MiB of HBM per device.

```python
import math
import jax
import jax.numpy as jnp
from jax import lax

NLEV = 72
SWEEPS = 12
NLAT = 128
NLON = 768


def touch_ends(values, rng, low, top_value):
    spot = [jax.random.randint(jax.random.fold_in(rng, axis), (), 0, length) for axis, length in enumerate(values.shape)]
    longest = values.shape.index(max(values.shape))
    next_to = spot[:longest] + [(spot[longest] + 1) % values.shape[longest]] + spot[longest + 1:]
    return values.at[tuple(spot)].set(low).at[tuple(next_to)].set(top_value)


def level_of(own_key, dims, cuts, smallest, high):
    def one(dim, parts):
        draws = jax.random.uniform(jax.random.fold_in(jax.random.fold_in(own_key, 6), dim), (parts,), jnp.float32, smallest / len(cuts), high / len(cuts))
        return jnp.repeat(jnp.exp(draws), dims[dim] // parts).reshape((-1,) + (1,) * (len(dims) - dim - 1))

    factor_of = one(*cuts[0])
    for cut in cuts[1:]:
        factor_of = factor_of * one(*cut)
    return factor_of


def gaussian(rng, dims, width, most, kind=jnp.bfloat16):
    values = width * jax.random.normal(rng, dims, jnp.float32)
    return jnp.clip(values, min=-most, max=most).astype(kind)


def setup_inputs(seed: int = 0, part: int = 0) -> dict:
    splits = jax.random.split(jax.random.key(seed), 6)
    part_splits = jax.random.split(jax.random.fold_in(splits[5], part), 6)
    return {
        "land_mask": touch_ends((jax.random.randint(splits[0], (NLEV, NLAT, NLON), 0, 4) < 3).astype(jnp.int32), jax.random.fold_in(splits[0], 1), 0, 1),
        "diffusivity": jnp.clip(jnp.exp(math.log(3.0) - 2.3025851 * jax.random.uniform(splits[1], (NLEV, NLAT, NLON), jnp.float32) ** level_of(splits[1], (NLEV, NLAT, NLON), ((0, 2), (1, 4), (2, 2)), -0.2, 0.2)), 0.3, 3.0),
        "balance": gaussian(splits[2], (NLEV, NLEV), NLEV ** -0.5, 0.75, jnp.float32),
        "member_id": jax.random.randint(part_splits[3], (1,), 0, 64).astype(jnp.int32),
        "counter_key": jax.random.randint(part_splits[4], (1,), 0, 1048576).astype(jnp.int32),
    }


noise_scale = math.sqrt(3.0) / 65536.0

def scramble(values):
    values = values * 1103515245 + 12345
    values = jnp.bitwise_xor(values, jnp.right_shift(values, 15))
    values = values * 747796405 + 1013904223
    values = jnp.bitwise_xor(values, jnp.right_shift(values, 13))
    values = values * 277803737
    return jnp.bitwise_xor(values, jnp.right_shift(values, 16))

def make_noise(level_ids, row_ids, col_ids, total_rows, total_cols, stream_base):
    global_index = (level_ids[:, None, None] * total_rows + row_ids[None, :, None]) * total_cols + col_ids[None, None, :]
    first = scramble(jnp.bitwise_xor(global_index, stream_base))
    second = scramble(first + 1664525)
    total = jnp.bitwise_and(first, 65535) + jnp.bitwise_and(jnp.right_shift(first, 16), 65535) + jnp.bitwise_and(second, 65535) + jnp.bitwise_and(jnp.right_shift(second, 16), 65535) - 131070
    return total.astype(jnp.float32) * noise_scale

def lat_prev(values):
    return jnp.pad(values, ((0, 0), (1, 0), (0, 0)))[:, :-1, :]

def lat_next(values):
    return jnp.pad(values, ((0, 0), (0, 1), (0, 0)))[:, 1:, :]

def reference(land_mask, diffusivity, balance, member_id, counter_key):
    stream_base = counter_key[0] * 69069 + member_id[0] * 362437
    level_ids = jnp.arange(NLEV, dtype=jnp.int32)
    row_ids = jnp.arange(NLAT, dtype=jnp.int32)
    col_ids = jnp.arange(NLON, dtype=jnp.int32)
    source = make_noise(level_ids, row_ids, col_ids, NLAT, NLON, stream_base)
    conduct = diffusivity * land_mask.astype(jnp.float32)
    north = conduct * lat_prev(conduct)
    south = conduct * lat_next(conduct)
    west = conduct * jnp.roll(conduct, 1, axis=2)
    east = conduct * jnp.roll(conduct, -1, axis=2)
    denom = 1.0 + (north + south + west + east)
    field = source
    for sweep_index in range(SWEEPS):
        field = (source + north * lat_prev(field) + south * lat_next(field) + west * jnp.roll(field, 1, axis=2) + east * jnp.roll(field, -1, axis=2)) / denom
    masked = field * land_mask.astype(jnp.float32)
    return jnp.einsum('lm,mrc->lrc', balance, masked, precision=lax.Precision.HIGHEST)
```

```python
import functools
import math

import jax
import jax.numpy as jnp
from jax import lax
from jax.experimental import pallas as pl
from jax.experimental.pallas import tpu as pltpu
from jax.sharding import PartitionSpec as P

SWEEPS = 12
noise_scale = math.sqrt(3.0) / 65536.0
LANES, SUB = 128, 8

def scramble(values):
    values = values * 1103515245 + 12345
    values = values ^ (values >> 15)
    values = values * 747796405 + 1013904223
    values = values ^ (values >> 13)
    values = values * 277803737
    return values ^ (values >> 16)

def draw(index, stream_base):
    first = scramble(index ^ stream_base)
    second = scramble(first + 1664525)
    total = ((first & 65535) + ((first >> 16) & 65535) + (second & 65535) + ((second >> 16) & 65535) - 131070)
    return total.astype(jnp.float32) * noise_scale

def noise_kernel(total_rows, total_cols, pitch, ids, out):
    levels, tiles = out.shape[0], out.shape[1]
    base, level0, row0 = ids[0], ids[1], ids[2]
    sub = lax.broadcasted_iota(jnp.int32, (SUB, LANES), 0)
    lane = lax.broadcasted_iota(jnp.int32, (SUB, LANES), 1)
    within = sub * (pitch * total_cols) + lane
    @pl.loop(0, levels)
    def _(l):
        start = ((level0 + l) * total_rows + row0) * total_cols
        for t in range(tiles):
            for k in range(pitch):
                out[l, t, k] = draw(within + (start + k * total_cols + t * LANES), base)

def neighbours(get, tiles, pitch, t, lane):
    here = [get(t, k) for k in range(pitch)]
    wt, et = (t - 1) % tiles, (t + 1) % tiles
    up = pltpu.roll(here[pitch - 1], 1, 0)
    down = pltpu.roll(here[0], SUB - 1, 0)
    sums = []
    for k in range(pitch):
        w = pltpu.roll(jnp.where(lane == LANES - 1, get(wt, k), here[k]), 1, 1)
        e = pltpu.roll(jnp.where(lane == 0, get(et, k), here[k]), LANES - 1, 1)
        n = here[k - 1] if k else up
        s = here[k + 1] if k < pitch - 1 else down
        sums.append((w + e) + (n + s))
    return here, sums

def diffuse_kernel(halo, own, top, bottom, source, out, rows, cond, gain, push, inv, u0, u1, res):
    tiles, pitch = source.shape[1], source.shape[2]
    height = own.shape[1]
    lane = lax.broadcasted_iota(jnp.int32, (SUB, LANES), 1)
    for t in range(tiles):
        cols = slice(t * LANES, (t + 1) * LANES)
        rows[t, pl.ds(0, halo), :] = top[0, :, cols]
        rows[t, pl.ds(halo, height), :] = own[0, :, cols]
        rows[t, pl.ds(halo + height, halo), :] = bottom[0, :, cols]
    for t in range(tiles):
        for k in range(pitch):
            cond[t, k] = rows[t, pl.ds(k, SUB, stride=pitch), :]
    for t in range(tiles):
        here, sums = neighbours(lambda a, b: cond[a, b], tiles, pitch, t, lane)
        for k in range(pitch):
            c, s = here[k], source[0, t, k]
            r = 1.0 / (1.0 + c * sums[k])
            q = c * r
            inv[t, k] = r
            push[t, k] = q * s
            gain[t, k] = q * c
            u0[t, k] = c * s
    def sweep(old, new):
        for t in range(tiles):
            _, sums = neighbours(lambda a, b: old[a, b], tiles, pitch, t, lane)
            for k in range(pitch):
                new[t, k] = push[t, k] + gain[t, k] * sums[k]
    @pl.loop(0, (SWEEPS - 2) // 2)
    def _(i):
        sweep(u0, u1)
        sweep(u1, u0)
    sweep(u0, u1)
    for t in range(tiles):
        _, sums = neighbours(lambda a, b: u1[a, b], tiles, pitch, t, lane)
        for k in range(pitch):
            c, s = cond[t, k], source[0, t, k]
            res[t, pl.ds(k, SUB, stride=pitch), :] = jnp.where(c != 0.0, (s + c * sums[k]) * inv[t, k], 0.0)
    for t in range(tiles):
        out[0, t] = res[t, pl.ds(halo, height), :]

def noise(ids, levels, tiles, pitch, total_rows, total_cols):
    return pl.pallas_call(
        functools.partial(noise_kernel, total_rows, total_cols, pitch),
        out_shape=jax.ShapeDtypeStruct((levels, tiles, pitch, SUB, LANES), jnp.float32),
        in_specs=[pl.BlockSpec(memory_space=pltpu.SMEM)],
        out_specs=pl.BlockSpec(memory_space=pltpu.VMEM),
    )(ids)

def diffuse(own, top, bottom, source):
    levels, height, width = own.shape
    halo = top.shape[1]
    tiles, pitch = source.shape[1:3]
    tile = pltpu.VMEM((tiles, pitch, SUB, LANES), jnp.float32)
    line = pltpu.VMEM((tiles, pitch * SUB, LANES), jnp.float32)
    return pl.pallas_call(
        functools.partial(diffuse_kernel, halo),
        out_shape=jax.ShapeDtypeStruct((levels, tiles, height, LANES), jnp.float32),
        grid=(levels,),
        in_specs=[pl.BlockSpec((1, height, width), lambda l: (l, 0, 0)),
                  pl.BlockSpec((1, halo, width), lambda l: (l, 0, 0)),
                  pl.BlockSpec((1, halo, width), lambda l: (l, 0, 0)),
                  pl.BlockSpec((1, tiles, pitch, SUB, LANES), lambda l: (l, 0, 0, 0, 0))],
        out_specs=pl.BlockSpec((1, tiles, height, LANES), lambda l: (l, 0, 0, 0)),
        scratch_shapes=[line] + [tile] * 6 + [line],
    )(own, top, bottom, source)


def balance_kernel(weights, own, other, out, columns, result):
    total, tiles, height = weights.shape[0], own.shape[1], own.shape[2]
    near, pitch = own.shape[0], tiles * height
    columns[0 : near * pitch, :] = own[...].reshape(near * pitch, LANES)
    columns[near * pitch :, :] = other[...].reshape(other.shape[0] * pitch, LANES)
    left = weights[...]
    high = left.astype(jnp.bfloat16)
    low = (left - high.astype(jnp.float32)).astype(jnp.bfloat16)
    stacked = jnp.concatenate([high, high, low], axis=1)
    for r in range(height):
        for t in range(tiles):
            column = columns[pl.ds(t * height + r, total, stride=pitch), :]
            top = column.astype(jnp.bfloat16)
            rest = (column - top.astype(jnp.float32)).astype(jnp.bfloat16)
            right = jnp.concatenate([top, rest, top], axis=0)
            result[pl.ds(t * height + r, total, stride=pitch), :] = jnp.dot(
                stacked, right, preferred_element_type=jnp.float32
            )
    for t in range(tiles):
        for l in range(total):
            start = l * pitch + t * height
            out[l, :, t * LANES : (t + 1) * LANES] = result[start : start + height, :]


def balanced(weights, own, other):
    tiles, height = own.shape[1:3]
    total = weights.shape[0]
    flat = pltpu.VMEM((total * tiles * height, LANES), jnp.float32)
    return pl.pallas_call(
        balance_kernel,
        out_shape=jax.ShapeDtypeStruct((total, height, tiles * LANES), jnp.float32),
        in_specs=[pl.BlockSpec(memory_space=pltpu.VMEM)] * 3,
        out_specs=pl.BlockSpec(memory_space=pltpu.VMEM),
        scratch_shapes=[flat, flat],
        compiler_params=pltpu.CompilerParams(vmem_limit_bytes=48 << 20),
    )(weights, own, other)


def swapped(keep, send, axis):
    count = lax.axis_size(axis)
    return keep, lax.ppermute(send, axis, [(i, count - 1 - i) for i in range(count)])


def part(block, index, size, axis):
    return lax.dynamic_slice_in_dim(block, index * size, size, axis=axis)


def per_device(land_mask, diffusivity, balance, member_id, counter_key):
    levels, height, breadth = land_mask.shape
    cores, groups, strips = (lax.axis_size(a) for a in ("lon", "lev", "lat"))
    core, group, strip = (lax.axis_index(a) for a in ("lon", "lev", "lat"))
    assert cores == 2 and height > SWEEPS
    halo = SWEEPS
    pitch = (height + 2 * halo) // SUB
    share = -(-levels // cores)
    conduct = diffusivity * land_mask.astype(jnp.float32)
    conduct = jnp.pad(conduct, ((0, share * cores - levels), (0, 0), (0, 0)))
    mine, theirs = swapped(part(conduct, core, share, 0), part(conduct, 1 - core, share, 0), "lon")
    own = jnp.concatenate([jnp.where(core == 0, mine, theirs), jnp.where(core == 0, theirs, mine)], axis=2)
    onward = [(i, i + 1) for i in range(strips - 1)]
    top = lax.ppermute(own[:, -halo:], "lat", onward)
    bottom = lax.ppermute(own[:, :halo], "lat", [(b, a) for a, b in onward])
    base = counter_key[0] * 69069 + member_id[0] * 362437
    ids = jnp.stack([base, group * levels + core * share, strip * height - halo])
    tiles = breadth * cores // LANES
    source = noise(ids, share, tiles, pitch, height * strips, breadth * cores)
    masked = diffuse(own, top, bottom, source)
    mine, theirs = swapped(part(masked, core, tiles // cores, 1), part(masked, 1 - core, tiles // cores, 1), "lon")
    column = jnp.concatenate([jnp.where(core == 0, mine, theirs), jnp.where(core == 0, theirs, mine)], axis=0)
    column = column[:levels]
    final = height // groups
    if groups == 2:
        near, far = swapped(part(column, group, final, 2), part(column, 1 - group, final, 2), "lev")
        weights = jnp.concatenate([part(balance, group, levels, 1), part(balance, 1 - group, levels, 1)], axis=1)
    else:
        near = lax.all_to_all(column, "lev", split_axis=2, concat_axis=0, tiled=True)
        near, far = near[: levels * groups // 2], near[levels * groups // 2 :]
        weights = balance
    return balanced(weights, near, far)


def solution(mesh):
    in_specs = (P("lev", "lat", "lon"), P("lev", "lat", "lon"), P(), P("member"), P("member"))
    out_specs = P("member", ("lat", "lev"), "lon")
    return jax.shard_map(
        per_device, mesh=mesh, in_specs=in_specs, out_specs=out_specs, check_vma=False
    )
```

```python
import functools
import math

import jax
import jax.numpy as jnp
from jax import lax
from jax.experimental import pallas as pl
from jax.experimental.pallas import tpu as pltpu
from jax.sharding import PartitionSpec as P

SWEEPS = 12
noise_scale = math.sqrt(3.0) / 65536.0
LANES, SUB = 128, 8
HALF = LANES // 2
VMEM = pltpu.VMEM
whole = functools.partial(pl.BlockSpec, memory_space=pltpu.VMEM)
scalars = functools.partial(pl.BlockSpec, memory_space=pltpu.SMEM)


def scramble(values):
    values = values * 1103515245 + 12345
    values = values ^ (values >> 15)
    values = values * 747796405 + 1013904223
    values = values ^ (values >> 13)
    values = values * 277803737
    return values ^ (values >> 16)


def draw(index, stream_base):
    first = scramble(index ^ stream_base)
    second = scramble(first + 1664525)
    total = (
        (first & 65535)
        + ((first >> 16) & 65535)
        + (second & 65535)
        + ((second >> 16) & 65535)
        - 131070
    )
    return total.astype(jnp.float32) * noise_scale


def packed_source(columns, tiles, core):
    lane = columns & (LANES - 1)
    tile = (columns // LANES) + (tiles // 2) * ((lane // HALF) ^ core)
    return (lane & (HALF - 1)) * tiles + tile


def packing(width, tiles, core, axis):
    natural = lax.broadcasted_iota(jnp.int32, (width, width), 1 - axis)
    columns = lax.broadcasted_iota(jnp.int32, (width, width), axis)
    return jnp.where(packed_source(columns, tiles, core) == natural, 1.0, 0.0).astype(jnp.bfloat16)


def split(values):
    high = values.astype(jnp.bfloat16)
    return high, (values - high.astype(jnp.float32)).astype(jnp.bfloat16)


def permuted(values, matrix):
    high, low = split(values)
    both = jnp.concatenate([high, low], axis=1)
    return jnp.dot(both, jnp.concatenate([matrix, matrix], axis=0), preferred_element_type=jnp.float32)


def conduct_kernel(ids, mask, diffusivity, out, matrix):
    levels, height, width = mask.shape
    tiles = 2 * width // LANES

    @pl.when(pl.program_id(0) == 0)
    def _():
        matrix[...] = packing(width, tiles, ids[0], 1)

    conduct = diffusivity[...] * mask[...].astype(jnp.float32)
    moved = permuted(conduct.reshape(levels * height, width), matrix[...])
    for t in range(width // LANES):
        out[:, t] = moved[:, t * LANES : (t + 1) * LANES].reshape(levels, height, LANES)


def packed_conduct(ids, mask, diffusivity):
    levels, height, width = mask.shape
    step = math.gcd(levels, 6)
    block = pl.BlockSpec((step, height, width), lambda l: (l, 0, 0))
    return pl.pallas_call(
        conduct_kernel,
        out_shape=jax.ShapeDtypeStruct((levels, width // LANES, height, LANES), jnp.float32),
        grid=(levels // step,),
        in_specs=[scalars(), block, block],
        out_specs=pl.BlockSpec((step, width // LANES, height, LANES), lambda l: (l, 0, 0, 0)),
        scratch_shapes=[VMEM((width, width), jnp.bfloat16)],
    )(ids, mask, diffusivity)


def noise_kernel(total_rows, total_cols, ids, out):
    levels, tiles, pitch = out.shape[:3]
    base, level0, row0 = ids[0], ids[1], ids[2]
    sub = lax.broadcasted_iota(jnp.int32, (SUB, LANES), 0)
    lane = lax.broadcasted_iota(jnp.int32, (SUB, LANES), 1)
    within = sub * (pitch * total_cols) + lane * tiles

    @pl.loop(0, levels)
    def _(l):
        start = ((level0 + l) * total_rows + row0) * total_cols
        for t in range(tiles):
            for k in range(pitch):
                out[l, t, k] = draw(within + (start + k * total_cols + t), base)


def noise(ids, levels, tiles, pitch, total_rows, total_cols):
    return pl.pallas_call(
        functools.partial(noise_kernel, total_rows, total_cols),
        out_shape=jax.ShapeDtypeStruct((levels, tiles, pitch, SUB, LANES), jnp.float32),
        in_specs=[scalars()],
        out_specs=whole(),
    )(ids)


def neighbour_sums(old, tiles, pitch, emit):
    first = [old[t, 0] for t in range(tiles)]
    last = [old[t, pitch - 1] for t in range(tiles)]
    above = [pltpu.roll(v, 1, 0) for v in last]
    here = first
    for k in range(pitch):
        if k == pitch - 1:
            below = [pltpu.roll(v, SUB - 1, 0) for v in first]
        elif k == pitch - 2:
            below = last
        else:
            below = [old[t, k + 1] for t in range(tiles)]
        west = [pltpu.roll(here[-1], 1, 1)] + here[:-1]
        east = here[1:] + [pltpu.roll(here[0], LANES - 1, 1)]
        for t in range(tiles):
            emit(t, k, here[t], (west[t] + east[t]) + (above[t] + below[t]))
        above, here = here, below


def diffuse_kernel(halo, ids, mine, theirs, top_mine, top_theirs, low_mine, low_theirs, source, near, far,
                   rows, cond, gain, push, inv, u0, u1, res):
    tiles, pitch = source.shape[1], source.shape[2]
    pairs, height = mine.shape[1], mine.shape[2]
    core, group = ids[0], ids[3]

    def on_left(shape):
        lane = lax.broadcasted_iota(jnp.int32, shape, len(shape) - 1)
        return (lane // HALF) == core

    for a, b, start in (
        (top_mine, top_theirs, 0), (mine, theirs, halo), (low_mine, low_theirs, halo + height),
    ):
        count = a.shape[2]
        left = on_left((count, LANES))
        for v in range(pairs):
            p, q = a[0, v], b[0, v]
            rows[v, pl.ds(start, count), :] = jnp.where(left, p, q)
            rows[v + pairs, pl.ds(start, count), :] = pltpu.roll(jnp.where(left, q, p), HALF, 1)
    for t in range(tiles):
        for k in range(pitch):
            cond[t, k] = rows[t, pl.ds(k, SUB, stride=pitch), :]

    def prepare(t, k, c, total):
        s = source[0, t, k]
        r = 1.0 / (1.0 + c * total)
        q = c * r
        inv[t, k] = r
        push[t, k] = q * s
        gain[t, k] = q * c
        u0[t, k] = c * s

    neighbour_sums(cond, tiles, pitch, prepare)

    def sweep(old, new):
        def step(t, k, value, total):
            new[t, k] = push[t, k] + gain[t, k] * total

        neighbour_sums(old, tiles, pitch, step)

    @pl.loop(0, (SWEEPS - 2) // 2)
    def _(i):
        sweep(u0, u1)
        sweep(u1, u0)

    sweep(u0, u1)

    def finish(t, k, value, total):
        c, s = cond[t, k], source[0, t, k]
        res[t, pl.ds(k, SUB, stride=pitch), :] = jnp.where(c != 0.0, (s + c * total) * inv[t, k], 0.0)

    neighbour_sums(u1, tiles, pitch, finish)
    left = on_left((height, LANES))
    final = height // 2
    for v in range(pairs):
        a = res[v, pl.ds(halo, height), :]
        b = pltpu.roll(res[v + pairs, pl.ds(halo, height), :], HALF, 1)
        keep, send = jnp.where(left, a, b), jnp.where(left, b, a)
        for value, slot in ((keep, 0), (send, 1)):
            upper, lower = value[:final], value[final:]
            first = group == 0
            near[slot, 0, v] = jnp.where(first, upper, lower)
            far[slot, 0, v] = jnp.where(first, lower, upper)


def diffuse(ids, mine, theirs, top, bottom, source):
    levels, pairs, height, _ = mine.shape
    halo = top.shape[3]
    tiles, pitch = source.shape[1:3]
    tile = VMEM((tiles, pitch, SUB, LANES), jnp.float32)
    line = VMEM((tiles, pitch * SUB, LANES), jnp.float32)
    own = pl.BlockSpec((1, pairs, height, LANES), lambda l: (l, 0, 0, 0))
    edge = [pl.BlockSpec((pl.Squeezed(), 1, pairs, halo, LANES), lambda l, i=i: (i, l, 0, 0, 0)) for i in range(2)]
    result = jax.ShapeDtypeStruct((2, levels, pairs, height // 2, LANES), jnp.float32)
    part = pl.BlockSpec((2, 1, pairs, height // 2, LANES), lambda l: (0, l, 0, 0, 0))
    return pl.pallas_call(
        functools.partial(diffuse_kernel, halo),
        out_shape=(result, result),
        grid=(levels,),
        in_specs=[scalars(), own, own, *edge, *edge,
                  pl.BlockSpec((1, tiles, pitch, SUB, LANES), lambda l: (l, 0, 0, 0, 0))],
        out_specs=(part, part),
        scratch_shapes=[line] + [tile] * 6 + [line],
    )(ids, mine, theirs, top, top, bottom, bottom, source)


def unpack(pieces, matrix, out, start):
    for piece in pieces:
        levels, tiles, height, _ = piece.shape
        values = jnp.concatenate(
            [piece[:, t].reshape(levels * height, LANES) for t in range(tiles)], axis=1
        )
        moved = permuted(values, matrix)
        for t in range(tiles):
            out[start : start + levels, t] = moved[:, t * LANES : (t + 1) * LANES].reshape(levels, height, LANES)
        start += levels


def unpack_kernel(ids, *refs):
    *pieces, out = refs
    tiles = pieces[0].shape[1]
    unpack(pieces, packing(tiles * LANES, 2 * tiles, ids[0], 0), out, 0)


def unpacked(ids, pieces):
    levels, tiles, height, _ = pieces[0].shape
    return pl.pallas_call(
        unpack_kernel,
        out_shape=jax.ShapeDtypeStruct((sum(p.shape[0] for p in pieces), tiles, height, LANES), jnp.float32),
        in_specs=[scalars()] + [whole()] * len(pieces),
        out_specs=whole(),
    )(ids, *pieces)


def balance_kernel(ids, weights, near, *refs):
    *pieces, out, columns, result = refs
    total = weights.shape[0]
    count, tiles, height, _ = columns.shape
    pitch = tiles * height
    columns[: near.shape[0]] = near[...]
    unpack(pieces, packing(tiles * LANES, 2 * tiles, ids[0], 0), columns, near.shape[0])
    flat = columns.reshape(count * pitch, LANES)
    high, low = split(weights[...])
    stacked = jnp.concatenate([high, high, low], axis=1)
    for r in range(height):
        for t in range(tiles):
            top, rest = split(flat[pl.ds(t * height + r, count, stride=pitch), :])
            right = jnp.concatenate([top, rest, top], axis=0)
            result[pl.ds(t * height + r, total, stride=pitch), :] = jnp.dot(
                stacked, right, preferred_element_type=jnp.float32
            )
    for t in range(tiles):
        for l in range(total):
            start = l * pitch + t * height
            out[l, :, t * LANES : (t + 1) * LANES] = result[start : start + height, :]


def balanced(ids, weights, near, pieces):
    _, tiles, height, _ = near.shape
    total, count = weights.shape
    return pl.pallas_call(
        balance_kernel,
        out_shape=jax.ShapeDtypeStruct((total, height, tiles * LANES), jnp.float32),
        in_specs=[scalars()] + [whole()] * (2 + len(pieces)),
        out_specs=whole(),
        scratch_shapes=[
            VMEM((count, tiles, height, LANES), jnp.float32),
            VMEM((total * tiles * height, LANES), jnp.float32),
        ],
        compiler_params=pltpu.CompilerParams(vmem_limit_bytes=48 << 20),
    )(ids, weights, near, *pieces)


def crossed(block, axis):
    count = lax.axis_size(axis)
    return lax.ppermute(block, axis, [(i, count - 1 - i) for i in range(count)])


def part(block, index, size, axis):
    return lax.dynamic_slice_in_dim(block, index * size, size, axis=axis)


def gathered(place, near, far, weights_of):
    core, groups = place[0], lax.axis_size("lev")
    rows = jnp.concatenate([near, far], axis=3)
    rows = jnp.stack([rows[0], crossed(rows[1], "lon")])
    pieces = lax.all_to_all(rows, "lev", split_axis=3, concat_axis=0, tiled=True)
    count, share, tiles, height, _ = pieces.shape
    values = pieces.transpose(0, 1, 3, 2, 4).reshape(count * share, height, tiles * LANES)
    matrix = packing(tiles * LANES, 2 * tiles, core, 0).astype(jnp.float32)
    values = jnp.einsum("mrp,pc->mrc", values, matrix, precision=lax.Precision.HIGHEST)
    weights = weights_of([(g, c) for g in range(groups) for c in (core, 1 - core)])
    return jnp.einsum("lm,mrc->lrc", weights, values, precision=lax.Precision.HIGHEST)


def per_device(land_mask, diffusivity, balance, member_id, counter_key):
    levels, height, breadth = land_mask.shape
    cores, groups, strips = (lax.axis_size(a) for a in ("lon", "lev", "lat"))
    core, group, strip = (lax.axis_index(a) for a in ("lon", "lev", "lat"))
    assert cores == 2 and height > SWEEPS
    halo = SWEEPS
    pitch = (height + 2 * halo) // SUB
    share = -(-levels // cores)
    spare = share * cores - levels
    if spare:
        land_mask, diffusivity = (jnp.pad(v, ((0, spare), (0, 0), (0, 0))) for v in (land_mask, diffusivity))
    base = counter_key[0] * 69069 + member_id[0] * 362437
    place = jnp.stack([core, core, core, group if groups == 2 else 0 * group])
    ids = jnp.stack([base, group * levels + core * share, strip * height - halo])
    conduct = packed_conduct(place, land_mask, diffusivity)
    mine, theirs = part(conduct, core, share, 0), crossed(part(conduct, 1 - core, share, 0), "lon")
    onward = [(i, i + 1) for i in range(strips - 1)]
    backward = [(b, a) for a, b in onward]
    edges = jnp.stack([mine, theirs])
    top = lax.ppermute(edges[:, :, :, -halo:], "lat", onward)
    bottom = lax.ppermute(edges[:, :, :, :halo], "lat", backward)
    tiles = breadth * cores // LANES
    source = noise(ids, share, tiles, pitch, height * strips, breadth * cores)
    near, far = diffuse(place, mine, theirs, top, bottom, source)

    def weights_of(order):
        padded = jnp.pad(balance.reshape(-1, groups, levels), ((0, 0), (0, 0), (0, spare)))
        padded = padded.reshape(-1, groups * cores * share)
        return jnp.concatenate([part(padded, g * cores + c, share, 1) for g, c in order], axis=1)

    if groups != 2:
        return gathered(place, near, far, weights_of)
    near_theirs = crossed(near[1], "lon")
    far_theirs = crossed(far[1], "lon")
    far_mine = crossed(far[0], "lev")
    far_theirs = crossed(far_theirs, "lev")
    weights = weights_of([(g, c) for g in (group, 1 - group) for c in (core, 1 - core)])
    own = unpacked(place, (near[0], near_theirs))
    return balanced(place, weights, own, (far_mine, far_theirs))


def solution(mesh):
    in_specs = (P("lev", "lat", "lon"), P("lev", "lat", "lon"), P(), P("member"), P("member"))
    out_specs = P("member", ("lat", "lev"), "lon")
    return jax.shard_map(
        per_device, mesh=mesh, in_specs=in_specs, out_specs=out_specs, check_vma=False
    )
```

```python
import functools
import math

import jax
import jax.numpy as jnp
from jax import lax
from jax.experimental import pallas as pl
from jax.experimental.pallas import tpu as pltpu
from jax.sharding import PartitionSpec as P

SWEEPS = 12
SOME = 3
noise_scale = math.sqrt(3.0) / 65536.0
LANES, SUB = 128, 8
HALF = LANES // 2
VMEM = pltpu.VMEM
whole = functools.partial(pl.BlockSpec, memory_space=pltpu.VMEM)
scalars = functools.partial(pl.BlockSpec, memory_space=pltpu.SMEM)


def scramble(values):
    values = values * 1103515245 + 12345
    values = values ^ (values >> 15)
    values = values * 747796405 + 1013904223
    values = values ^ (values >> 13)
    values = values * 277803737
    return values ^ (values >> 16)


def draw(index, stream_base):
    first = scramble(index ^ stream_base)
    second = scramble(first + 1664525)
    total = (
        (first & 65535)
        + ((first >> 16) & 65535)
        + (second & 65535)
        + ((second >> 16) & 65535)
        - 131070
    )
    return total.astype(jnp.float32) * noise_scale


def packed_source(columns, tiles, core):
    lane = columns & (LANES - 1)
    tile = (columns // LANES) + (tiles // 2) * ((lane // HALF) ^ core)
    return (lane & (HALF - 1)) * tiles + tile


def packing(width, tiles, core, axis):
    natural = lax.broadcasted_iota(jnp.int32, (width, width), 1 - axis)
    columns = lax.broadcasted_iota(jnp.int32, (width, width), axis)
    return jnp.where(packed_source(columns, tiles, core) == natural, 1.0, 0.0).astype(jnp.bfloat16)


def split(values):
    high = values.astype(jnp.bfloat16)
    return high, (values - high.astype(jnp.float32)).astype(jnp.bfloat16)


def permuted(values, matrix):
    rows = values.shape[0]
    both = jnp.dot(jnp.concatenate(split(values), axis=0), matrix, preferred_element_type=jnp.float32)
    return both[:rows] + both[rows:]


def quarter(keep):
    core = lax.axis_index("lon")
    return lax.axis_index("member") * 2 + (core if keep else 1 - core)


def edge_rows(some, pairs, halo):
    return -(-some * pairs * halo // SUB) * SUB


def conduct_kernel(halo, mask_mine, mine_in, mask_send, send_in, *refs):
    *outs, matrix = refs
    levels, height, width = mask_mine.shape
    pairs = width // LANES

    @pl.when(pl.program_id(0) == 0)
    def _():
        matrix[...] = packing(width, 2 * pairs, lax.axis_index("lon"), 1)

    both = [d[...] * m[...].astype(jnp.float32) for m, d in ((mask_mine, mine_in), (mask_send, send_in))]
    values = jnp.concatenate([v.reshape(levels * height, width) for v in both], axis=0)
    moved = permuted(values, matrix[...])
    for i in range(2):
        rows, top, bottom = outs[i], outs[2 + i], outs[4 + i]
        for g in range(levels):
            for v in range(pairs):
                start = (i * levels + g) * height
                value = moved[start : start + height, v * LANES : (v + 1) * LANES]
                rows[g, v] = value
                here = pl.ds((g * pairs + v) * halo, halo)
                top[0, here, :] = value[height - halo :]
                bottom[0, here, :] = value[:halo]


def packed_conduct(halo, share, mask, diffusivity):
    _, height, width = mask.shape
    some, pairs = math.gcd(share, SOME), width // LANES
    steps = share // some
    extent = edge_rows(some, pairs, halo)
    ins = [
        pl.BlockSpec((some, height, width), lambda l, keep=keep: (quarter(keep) * steps + l, 0, 0))
        for keep in (True, True, False, False)
    ]
    rows = jax.ShapeDtypeStruct((share, pairs, height, LANES), jnp.float32)
    edge = jax.ShapeDtypeStruct((steps, extent, LANES), jnp.float32)
    return pl.pallas_call(
        functools.partial(conduct_kernel, halo),
        out_shape=(rows,) * 2 + (edge,) * 4,
        grid=(steps,),
        in_specs=ins,
        out_specs=[pl.BlockSpec((some, pairs, height, LANES), lambda l: (l, 0, 0, 0))] * 2
        + [pl.BlockSpec((1, extent, LANES), lambda l: (l, 0, 0))] * 4,
        scratch_shapes=[VMEM((width, width), jnp.bfloat16)],
    )(mask, diffusivity, mask, diffusivity)


def noise_kernel(levels_here, halo, total_rows, total_cols, key, member, out):
    levels, tiles, pitch = out.shape[:3]
    base = key[0] * 69069 + member[0] * 362437
    level0 = lax.axis_index("lev") * levels_here + quarter(True) * levels
    row0 = lax.axis_index("lat") * (total_rows // lax.axis_size("lat")) - halo
    sub = lax.broadcasted_iota(jnp.int32, (SUB, LANES), 0)
    lane = lax.broadcasted_iota(jnp.int32, (SUB, LANES), 1)
    within = sub * (pitch * total_cols) + lane * tiles

    @pl.loop(0, levels)
    def _(l):
        start = ((level0 + l) * total_rows + row0) * total_cols
        for t in range(tiles):
            for k in range(pitch):
                out[l, t, k] = draw(within + (start + k * total_cols + t), base)


def noise(key, member, levels_here, halo, shape, total_rows, total_cols):
    return pl.pallas_call(
        functools.partial(noise_kernel, levels_here, halo, total_rows, total_cols),
        out_shape=jax.ShapeDtypeStruct(shape, jnp.float32),
        in_specs=[scalars()] * 2,
        out_specs=whole(),
    )(key, member)


def neighbour_sums(old, tiles, pitch, emit):
    some = range(old.shape[0])
    first = [[old[g, t, 0] for t in range(tiles)] for g in some]
    last = [[old[g, t, pitch - 1] for t in range(tiles)] for g in some]
    above = [[pltpu.roll(v, 1, 0) for v in last[g]] for g in some]
    here = first
    for k in range(pitch):
        if k == pitch - 1:
            below = [[pltpu.roll(v, SUB - 1, 0) for v in first[g]] for g in some]
        elif k == pitch - 2:
            below = last
        else:
            below = [[old[g, t, k + 1] for t in range(tiles)] for g in some]
        for g in some:
            row = here[g]
            west = [pltpu.roll(row[-1], 1, 1)] + row[:-1]
            east = row[1:] + [pltpu.roll(row[0], LANES - 1, 1)]
            for t in ORDER(tiles):
                emit(g, t, k, row[t], (west[t] + east[t]) + (above[g][t] + below[g][t]))
        above, here = here, below


def ORDER(tiles):
    return [*range(1, tiles - 1), 0, tiles - 1]


def diffuse_kernel(halo, halves, mine, theirs, top_mine, top_theirs, bottom_mine, bottom_theirs,
                   other_source, own_source, *refs):
    outs, (rows, cond, gain, push, inv, u0, u1, res) = refs[:8], refs[8:]
    sources = (other_source, own_source)
    levels, tiles, pitch = own_source.shape[:3]
    pairs, height = mine.shape[1], mine.shape[2]
    final = height // 2
    core = lax.axis_index("lon")
    group = lax.axis_index("lev") if halves else 0
    some = cond.shape[0]

    def on_left(shape):
        lane = lax.broadcasted_iota(jnp.int32, shape, len(shape) - 1)
        return (lane // HALF) == core

    def sweep(old, new):
        def step(g, t, k, value, total):
            new[g, t, k] = push[g, t, k] + gain[g % some, t, k] * total

        neighbour_sums(old, tiles, pitch, step)

    @pl.loop(0, levels // some)
    def _(block):
        for g in range(some):
            l = block * some + g
            for v in range(pairs):
                edge = pl.ds((g * pairs + v) * halo, halo)
                for p, q, start in (
                    (top_mine[block, edge, :], top_theirs[block, edge, :], 0),
                    (mine[l, v], theirs[l, v], halo),
                    (bottom_mine[block, edge, :], bottom_theirs[block, edge, :], halo + height),
                ):
                    count = p.shape[0]
                    left = on_left(p.shape)
                    rows[g, v, pl.ds(start, count), :] = jnp.where(left, p, q)
                    rows[g, v + pairs, pl.ds(start, count), :] = pltpu.roll(jnp.where(left, q, p), HALF, 1)
            for t in range(tiles):
                for k in range(pitch):
                    cond[g, t, k] = rows[g, t, pl.ds(k, SUB, stride=pitch), :]

        def prepare(g, t, k, c, total):
            r = 1.0 / (1.0 + c * total)
            q = c * r
            inv[g, t, k] = r
            gain[g, t, k] = q * c
            for i, source in enumerate(sources):
                s = source[block * some + g, t, k]
                push[i * some + g, t, k] = q * s
                u0[i * some + g, t, k] = c * s

        neighbour_sums(cond, tiles, pitch, prepare)

        @pl.loop(0, (SWEEPS - 2) // 2)
        def _(i):
            sweep(u0, u1)
            sweep(u1, u0)

        sweep(u0, u1)

        def finish(g, t, k, value, total):
            i, g = divmod(g, some)
            c, s = cond[g, t, k], sources[i][block * some + g, t, k]
            value = jnp.where(c != 0.0, (s + c * total) * inv[g, t, k], 0.0)
            res[i * some + g, t, pl.ds(k, SUB, stride=pitch), :] = value

        neighbour_sums(u1, tiles, pitch, finish)
        left = on_left((height, LANES))
        first = group == 0
        for i in range(2):
            near, far, near_send, far_send = outs[4 * i : 4 * i + 4]
            for g in range(some):
                l = block * some + g
                for v in range(pairs):
                    a = res[i * some + g, v, pl.ds(halo, height), :]
                    b = pltpu.roll(res[i * some + g, v + pairs, pl.ds(halo, height), :], HALF, 1)
                    keep, send = jnp.where(left, a, b), jnp.where(left, b, a)
                    for value, close, away in ((keep, near, far), (send, near_send, far_send)):
                        upper, lower = value[:final], value[final:]
                        close[l, v] = jnp.where(first, upper, lower)
                        away[l, v] = jnp.where(first, lower, upper)


def diffuse(halo, halves, *operands):
    levels, pairs, height, _ = operands[0].shape
    tiles, pitch = operands[-1].shape[1:3]
    some = math.gcd(levels, SOME)
    tile = VMEM((some, tiles, pitch, SUB, LANES), jnp.float32)
    both = VMEM((2 * some, tiles, pitch, SUB, LANES), jnp.float32)
    line = VMEM((2 * some, tiles, pitch * SUB, LANES), jnp.float32)
    result = jax.ShapeDtypeStruct((levels, pairs, height // 2, LANES), jnp.float32)
    return pl.pallas_call(
        functools.partial(diffuse_kernel, halo, halves),
        out_shape=(result,) * 8,
        in_specs=[whole()] * len(operands),
        out_specs=(whole(),) * 8,
        scratch_shapes=[line, tile, tile, both, tile, both, both, line],
    )(*operands)


def unpack(pieces, matrix, out, start):
    for piece in pieces:
        levels, tiles, height, _ = piece.shape
        values = jnp.concatenate(
            [piece[:, t].reshape(levels * height, LANES) for t in range(tiles)], axis=1
        )
        moved = permuted(values, matrix)
        for t in range(tiles):
            out[start : start + levels, t] = moved[:, t * LANES : (t + 1) * LANES].reshape(levels, height, LANES)
        start += levels


def unpack_kernel(*refs):
    *pieces, out = refs
    tiles = pieces[0].shape[1]
    unpack(pieces, packing(tiles * LANES, 2 * tiles, lax.axis_index("lon"), 0), out, 0)


def unpacked(pieces):
    levels, tiles, height, _ = pieces[0].shape
    return pl.pallas_call(
        unpack_kernel,
        out_shape=jax.ShapeDtypeStruct((sum(p.shape[0] for p in pieces), tiles, height, LANES), jnp.float32),
        in_specs=[whole()] * len(pieces),
        out_specs=whole(),
    )(*pieces)


def balance_kernel(weights, near, *refs):
    *pieces, out, columns, result = refs
    total = weights.shape[0]
    count, tiles, height, _ = columns.shape
    pitch = tiles * height
    columns[: near.shape[0]] = near[...]
    unpack(pieces, packing(tiles * LANES, 2 * tiles, lax.axis_index("lon"), 0), columns, near.shape[0])
    flat = columns.reshape(count * pitch, LANES)
    high, low = split(weights[...])
    stacked = jnp.concatenate([high, high, low], axis=1)
    for r in range(height):
        for t in range(tiles):
            top, rest = split(flat[pl.ds(t * height + r, count, stride=pitch), :])
            right = jnp.concatenate([top, rest, top], axis=0)
            result[pl.ds(t * height + r, total, stride=pitch), :] = jnp.dot(
                stacked, right, preferred_element_type=jnp.float32
            )
    for t in range(tiles):
        for l in range(total):
            start = l * pitch + t * height
            out[l, :, t * LANES : (t + 1) * LANES] = result[start : start + height, :]


def balanced(weights, near, pieces):
    _, tiles, height, _ = near.shape
    total, count = weights.shape
    return pl.pallas_call(
        balance_kernel,
        out_shape=jax.ShapeDtypeStruct((total, height, tiles * LANES), jnp.float32),
        in_specs=[whole()] * (2 + len(pieces)),
        out_specs=whole(),
        scratch_shapes=[
            VMEM((count, tiles, height, LANES), jnp.float32),
            VMEM((total * tiles * height, LANES), jnp.float32),
        ],
        compiler_params=pltpu.CompilerParams(vmem_limit_bytes=48 << 20),
    )(weights, near, *pieces)


def crossed(block, *axes):
    count = math.prod(lax.axis_size(a) for a in axes)
    return lax.ppermute(block, axes, [(i, count - 1 - i) for i in range(count)])


def shifted(block, step, cross):
    strips = lax.axis_size("lat")
    route = [
        (2 * i + c, 2 * (i + step) + (1 - c if cross else c))
        for i in range(strips) if 0 <= i + step < strips for c in range(2)
    ]
    return lax.ppermute(block, ("lat", "lon"), route)


def part(block, index, size, axis):
    return lax.dynamic_slice_in_dim(block, index * size, size, axis=axis)


def gathered(kept, came, weights_of):
    core, member, groups = (lax.axis_index("lon"), lax.axis_index("member"), lax.axis_size("lev"))
    halves = [jnp.concatenate(half, axis=2) for half in (kept[2:], came[2:], kept[:2], came[:2])]
    rows = jnp.concatenate([jnp.stack(halves[:2]), crossed(jnp.stack(halves[2:]), "member")])
    pieces = lax.all_to_all(rows, "lev", split_axis=3, concat_axis=0, tiled=True)
    count, share, tiles, height, _ = pieces.shape
    values = pieces.transpose(0, 1, 3, 2, 4).reshape(count * share, height, tiles * LANES)
    matrix = packing(tiles * LANES, 2 * tiles, core, 0).astype(jnp.float32)
    values = jnp.einsum("mrp,pc->mrc", values, matrix, precision=lax.Precision.HIGHEST)
    weights = weights_of(
        [(g, m, c) for g in range(groups) for m in (member, 1 - member) for c in (core, 1 - core)]
    )
    return jnp.einsum("lm,mrc->lrc", weights, values, precision=lax.Precision.HIGHEST)


def per_device(land_mask, diffusivity, balance, member_id, counter_key):
    levels, height, breadth = land_mask.shape
    members, cores, groups, strips = (lax.axis_size(a) for a in ("member", "lon", "lev", "lat"))
    core, member, group = (lax.axis_index(a) for a in ("lon", "member", "lev"))
    assert members == 2 and cores == 2 and height > SWEEPS
    halo = SWEEPS
    pitch = (height + 2 * halo) // SUB
    share = -(-levels // 4)
    spare = share * 4 - levels
    if spare:
        land_mask, diffusivity = (jnp.pad(v, ((0, spare), (0, 0), (0, 0))) for v in (land_mask, diffusivity))
    mine, send, top, top_cross, bottom, bottom_cross = packed_conduct(halo, share, land_mask, diffusivity)
    top, bottom = shifted(top, 1, False), shifted(bottom, -1, False)
    top_cross, bottom_cross = shifted(top_cross, 1, True), shifted(bottom_cross, -1, True)
    theirs = crossed(send, "lon")
    tiles = breadth * cores // LANES
    sizes = (levels, halo, (share, tiles, pitch, SUB, LANES), height * strips, breadth * cores)
    own = noise(counter_key, member_id, *sizes)
    other = noise(crossed(counter_key, "member"), crossed(member_id, "member"), *sizes)
    outs = diffuse(halo, groups == 2, mine, theirs, top, top_cross, bottom, bottom_cross, other, own)

    def weights_of(order):
        padded = jnp.pad(balance.reshape(-1, groups, levels), ((0, 0), (0, 0), (0, spare)))
        padded = padded.reshape(-1, groups * 4 * share)
        return jnp.concatenate([part(padded, g * 4 + m * 2 + c, share, 1) for g, m, c in order], axis=1)

    other_near, other_far, other_near_send, other_far_send, near, far, near_send, far_send = outs
    came = [crossed(v, "lon") for v in (other_near_send, other_far_send, near_send, far_send)]
    if groups != 2:
        return gathered((other_near, other_far, near, far), came, weights_of)
    here = (near, came[2])
    along_x = [crossed(v, "lev") for v in (far, came[3])]
    along_y = [crossed(v, "member") for v in (other_near, came[0])]
    diagonal = [crossed(v, "member", "lev") for v in (other_far, came[1])]
    places = [(group, member), (group, 1 - member), (1 - group, 1 - member), (1 - group, member)]
    weights = weights_of([(g, m, c) for g, m in places for c in (core, 1 - core)])
    near = unpacked((*here, *along_y))
    return balanced(weights, near, (*diagonal, *along_x))


def solution(mesh):
    in_specs = (P("lev", "lat", "lon"), P("lev", "lat", "lon"), P(), P("member"), P("member"))
    out_specs = P("member", ("lat", "lev"), "lon")
    return jax.shard_map(
        per_device, mesh=mesh, in_specs=in_specs, out_specs=out_specs, check_vma=False
    )
```

```python
import functools
import math

import jax
import jax.numpy as jnp
from jax import lax
from jax.experimental import pallas as pl
from jax.experimental.pallas import tpu as pltpu
from jax.sharding import PartitionSpec as P

SWEEPS = 12
SOME = 3
noise_scale = math.sqrt(3.0) / 65536.0
LANES, SUB = 128, 8
HALF = LANES // 2
VMEM = pltpu.VMEM
whole = functools.partial(pl.BlockSpec, memory_space=pltpu.VMEM)
scalars = functools.partial(pl.BlockSpec, memory_space=pltpu.SMEM)


def budget(mebibytes):
    return pltpu.CompilerParams(vmem_limit_bytes=mebibytes << 20)


def scramble(values):
    values = values * 1103515245 + 12345
    values = values ^ (values >> 15)
    values = values * 747796405 + 1013904223
    values = values ^ (values >> 13)
    values = values * 277803737
    return values ^ (values >> 16)


def draw(index, stream_base):
    first = scramble(index ^ stream_base)
    second = scramble(first + 1664525)
    total = (
        (first & 65535)
        + ((first >> 16) & 65535)
        + (second & 65535)
        + ((second >> 16) & 65535)
        - 131070
    )
    return total.astype(jnp.float32) * noise_scale


def packed_source(columns, tiles, core):
    lane = columns & (LANES - 1)
    tile = (columns // LANES) + (tiles // 2) * ((lane // HALF) ^ core)
    return (lane & (HALF - 1)) * tiles + tile


def packing(width, tiles, core, axis):
    natural = lax.broadcasted_iota(jnp.int32, (width, width), 1 - axis)
    columns = lax.broadcasted_iota(jnp.int32, (width, width), axis)
    return jnp.where(packed_source(columns, tiles, core) == natural, 1.0, 0.0).astype(jnp.bfloat16)


def split(values):
    high = values.astype(jnp.bfloat16)
    return high, (values - high.astype(jnp.float32)).astype(jnp.bfloat16)


def permuted(values, matrix):
    rows = values.shape[0]
    both = jnp.dot(jnp.concatenate(split(values), axis=0), matrix, preferred_element_type=jnp.float32)
    return both[:rows] + both[rows:]


def quarter(keep):
    core = lax.axis_index("lon")
    return lax.axis_index("member") * 2 + (core if keep else 1 - core)


def edge_rows(some, pairs, halo):
    return -(-some * pairs * halo // SUB) * SUB


def conduct_kernel(halo, mask_mine, mine_in, mask_send, send_in, *refs):
    *outs, matrix = refs
    levels, height, width = mask_mine.shape
    pairs = width // LANES

    @pl.when(pl.program_id(0) == 0)
    def _():
        matrix[...] = packing(width, 2 * pairs, lax.axis_index("lon"), 1)

    both = [d[...] * m[...].astype(jnp.float32) for m, d in ((mask_mine, mine_in), (mask_send, send_in))]
    values = jnp.concatenate([v.reshape(levels * height, width) for v in both], axis=0)
    moved = permuted(values, matrix[...])
    for i in range(2):
        rows, top, bottom = outs[i], outs[2 + i], outs[4 + i]
        for g in range(levels):
            for v in range(pairs):
                start = (i * levels + g) * height
                value = moved[start : start + height, v * LANES : (v + 1) * LANES]
                rows[g, v] = value
                here = pl.ds((g * pairs + v) * halo, halo)
                top[0, here, :] = value[height - halo :]
                bottom[0, here, :] = value[:halo]


def packed_conduct(halo, share, mask, diffusivity):
    _, height, width = mask.shape
    some, pairs = math.gcd(share, SOME), width // LANES
    steps = share // some
    extent = edge_rows(some, pairs, halo)
    ins = [
        pl.BlockSpec((some, height, width), lambda l, keep=keep: (quarter(keep) * steps + l, 0, 0))
        for keep in (True, True, False, False)
    ]
    rows = jax.ShapeDtypeStruct((share, pairs, height, LANES), jnp.float32)
    edge = jax.ShapeDtypeStruct((steps, extent, LANES), jnp.float32)
    return pl.pallas_call(
        functools.partial(conduct_kernel, halo),
        out_shape=(rows,) * 2 + (edge,) * 4,
        grid=(steps,),
        in_specs=ins,
        out_specs=[pl.BlockSpec((some, pairs, height, LANES), lambda l: (l, 0, 0, 0))] * 2
        + [pl.BlockSpec((1, extent, LANES), lambda l: (l, 0, 0))] * 4,
        scratch_shapes=[VMEM((width, width), jnp.bfloat16)],
        compiler_params=budget(12),
    )(mask, diffusivity, mask, diffusivity)


def noise_kernel(levels_here, halo, total_rows, total_cols, other, own, out):
    _, levels, tiles, pitch = out.shape[:4]
    level0 = lax.axis_index("lev") * levels_here + quarter(True) * levels
    row0 = lax.axis_index("lat") * (total_rows // lax.axis_size("lat")) - halo
    sub = lax.broadcasted_iota(jnp.int32, (SUB, LANES), 0)
    lane = lax.broadcasted_iota(jnp.int32, (SUB, LANES), 1)
    within = sub * (pitch * total_cols) + lane * tiles
    bases = [ids[0] * 69069 + ids[1] * 362437 for ids in (other, own)]

    @pl.loop(0, levels)
    def _(l):
        start = ((level0 + l) * total_rows + row0) * total_cols
        for i, base in enumerate(bases):
            for t in range(tiles):
                for k in range(pitch):
                    out[i, l, t, k] = draw(within + (start + k * total_cols + t), base)


def noise(other, own, levels_here, halo, shape, total_rows, total_cols):
    return pl.pallas_call(
        functools.partial(noise_kernel, levels_here, halo, total_rows, total_cols),
        out_shape=jax.ShapeDtypeStruct((2, *shape), jnp.float32),
        in_specs=[scalars()] * 2,
        out_specs=whole(),
        compiler_params=budget(8),
    )(other, own)


def neighbour_sums(old, tiles, pitch, emit):
    some = range(old.shape[0])
    first = [[old[g, t, 0] for t in range(tiles)] for g in some]
    last = [[old[g, t, pitch - 1] for t in range(tiles)] for g in some]
    above = [[pltpu.roll(v, 1, 0) for v in last[g]] for g in some]
    here = first
    for k in range(pitch):
        if k == pitch - 1:
            below = [[pltpu.roll(v, SUB - 1, 0) for v in first[g]] for g in some]
        elif k == pitch - 2:
            below = last
        else:
            below = [[old[g, t, k + 1] for t in range(tiles)] for g in some]
        for g in some:
            row = here[g]
            west = [pltpu.roll(row[-1], 1, 1)] + row[:-1]
            east = row[1:] + [pltpu.roll(row[0], LANES - 1, 1)]
            for t in ORDER(tiles):
                emit(g, t, k, row[t], (west[t] + east[t]) + (above[g][t] + below[g][t]))
        above, here = here, below


def ORDER(tiles):
    return [*range(1, tiles - 1), 0, tiles - 1]


def diffuse_kernel(halo, halves, mine, theirs, top_mine, top_theirs, bottom_mine, bottom_theirs,
                   source, *refs):
    *kept, sent, rows, cond, gain, push, inv, u0, u1, res = refs
    _, levels, tiles, pitch = source.shape[:4]
    pairs, height = mine.shape[1], mine.shape[2]
    final = height // 2
    core = lax.axis_index("lon")
    group = lax.axis_index("lev") if halves else 0
    some = cond.shape[0]

    def on_left(shape):
        lane = lax.broadcasted_iota(jnp.int32, shape, len(shape) - 1)
        return (lane // HALF) == core

    def sweep(old, new):
        def step(g, t, k, value, total):
            new[g, t, k] = push[g, t, k] + gain[g % some, t, k] * total

        neighbour_sums(old, tiles, pitch, step)

    @pl.loop(0, levels // some)
    def _(block):
        for g in range(some):
            l = block * some + g
            for v in range(pairs):
                edge = pl.ds((g * pairs + v) * halo, halo)
                for p, q, start in (
                    (top_mine[block, edge, :], top_theirs[block, edge, :], 0),
                    (mine[l, v], theirs[l, v], halo),
                    (bottom_mine[block, edge, :], bottom_theirs[block, edge, :], halo + height),
                ):
                    count = p.shape[0]
                    left = on_left(p.shape)
                    rows[g, v, pl.ds(start, count), :] = jnp.where(left, p, q)
                    rows[g, v + pairs, pl.ds(start, count), :] = pltpu.roll(jnp.where(left, q, p), HALF, 1)
            for t in range(tiles):
                for k in range(pitch):
                    cond[g, t, k] = rows[g, t, pl.ds(k, SUB, stride=pitch), :]

        def prepare(g, t, k, c, total):
            r = 1.0 / (1.0 + c * total)
            q = c * r
            inv[g, t, k] = r
            gain[g, t, k] = q * c
            for i in range(2):
                s = source[i, block * some + g, t, k]
                push[i * some + g, t, k] = q * s
                u0[i * some + g, t, k] = c * s

        neighbour_sums(cond, tiles, pitch, prepare)

        @pl.loop(0, (SWEEPS - 2) // 2)
        def _(i):
            sweep(u0, u1)
            sweep(u1, u0)

        sweep(u0, u1)

        def finish(g, t, k, value, total):
            i, g = divmod(g, some)
            c, s = cond[g, t, k], source[i, block * some + g, t, k]
            value = jnp.where(c != 0.0, (s + c * total) * inv[g, t, k], 0.0)
            res[i * some + g, t, pl.ds(k, SUB, stride=pitch), :] = value

        neighbour_sums(u1, tiles, pitch, finish)
        left = on_left((height, LANES))
        first = group == 0
        for i in range(2):
            for g in range(some):
                l = block * some + g
                for v in range(pairs):
                    a = res[i * some + g, v, pl.ds(halo, height), :]
                    b = pltpu.roll(res[i * some + g, v + pairs, pl.ds(halo, height), :], HALF, 1)
                    keep, send = jnp.where(left, a, b), jnp.where(left, b, a)
                    for value, close, away in (
                        (keep, kept[2 * i], kept[2 * i + 1]), (send, sent.at[2 * i], sent.at[2 * i + 1]),
                    ):
                        upper, lower = value[:final], value[final:]
                        close[l, v] = jnp.where(first, upper, lower)
                        away[l, v] = jnp.where(first, lower, upper)


def diffuse(halo, halves, *operands):
    levels, pairs, height, _ = operands[0].shape
    tiles, pitch = operands[-1].shape[2:4]
    some = math.gcd(levels, SOME)
    tile = VMEM((some, tiles, pitch, SUB, LANES), jnp.float32)
    both = VMEM((2 * some, tiles, pitch, SUB, LANES), jnp.float32)
    line = VMEM((2 * some, tiles, pitch * SUB, LANES), jnp.float32)
    result = jax.ShapeDtypeStruct((levels, pairs, height // 2, LANES), jnp.float32)
    return pl.pallas_call(
        functools.partial(diffuse_kernel, halo, halves),
        out_shape=(result,) * 4 + (jax.ShapeDtypeStruct((4, *result.shape), jnp.float32),),
        in_specs=[whole()] * len(operands),
        out_specs=(whole(),) * 5,
        scratch_shapes=[line, tile, tile, both, tile, both, both, line],
        compiler_params=budget(18),
    )(*operands)


def unpack(pieces, matrix, out, start):
    for piece in (p.at[i] for p in pieces for i in range(2)):
        levels, tiles, height, _ = piece.shape
        values = jnp.concatenate(
            [piece[:, t].reshape(levels * height, LANES) for t in range(tiles)], axis=1
        )
        moved = permuted(values, matrix)
        for t in range(tiles):
            out[start : start + levels, t] = moved[:, t * LANES : (t + 1) * LANES].reshape(levels, height, LANES)
        start += levels


def unpack_kernel(*refs):
    *pieces, out = refs
    tiles = pieces[0].shape[2]
    unpack(pieces, packing(tiles * LANES, 2 * tiles, lax.axis_index("lon"), 0), out, 0)


def unpacked(pieces):
    _, levels, tiles, height, _ = pieces[0].shape
    return pl.pallas_call(
        unpack_kernel,
        out_shape=jax.ShapeDtypeStruct((2 * len(pieces) * levels, tiles, height, LANES), jnp.float32),
        in_specs=[whole()] * len(pieces),
        out_specs=whole(),
        compiler_params=budget(8),
    )(*pieces)


def balance_kernel(weights, near, *refs):
    *pieces, out, columns, result = refs
    total = weights.shape[0]
    count, tiles, height, _ = columns.shape
    pitch = tiles * height
    columns[: near.shape[0]] = near[...]
    unpack(pieces, packing(tiles * LANES, 2 * tiles, lax.axis_index("lon"), 0), columns, near.shape[0])
    flat = columns.reshape(count * pitch, LANES)
    high, low = split(weights[...])
    stacked = jnp.concatenate([high, high, low], axis=1)
    for r in range(height):
        for t in range(tiles):
            top, rest = split(flat[pl.ds(t * height + r, count, stride=pitch), :])
            right = jnp.concatenate([top, rest, top], axis=0)
            result[pl.ds(t * height + r, total, stride=pitch), :] = jnp.dot(
                stacked, right, preferred_element_type=jnp.float32
            )
    for t in range(tiles):
        for l in range(total):
            start = l * pitch + t * height
            out[l, :, t * LANES : (t + 1) * LANES] = result[start : start + height, :]


def balanced(weights, near, pieces):
    _, tiles, height, _ = near.shape
    total, count = weights.shape
    return pl.pallas_call(
        balance_kernel,
        out_shape=jax.ShapeDtypeStruct((total, height, tiles * LANES), jnp.float32),
        in_specs=[whole()] * (2 + len(pieces)),
        out_specs=whole(),
        scratch_shapes=[
            VMEM((count, tiles, height, LANES), jnp.float32),
            VMEM((total * tiles * height, LANES), jnp.float32),
        ],
        compiler_params=budget(12),
    )(weights, near, *pieces)


def crossed(block, *axes):
    count = math.prod(lax.axis_size(a) for a in axes)
    return lax.ppermute(block, axes, [(i, count - 1 - i) for i in range(count)])


def shifted(block, step, cross):
    strips = lax.axis_size("lat")
    route = [
        (2 * i + c, 2 * (i + step) + (1 - c if cross else c))
        for i in range(strips) if 0 <= i + step < strips for c in range(2)
    ]
    return lax.ppermute(block, ("lat", "lon"), route)


def part(block, index, size, axis):
    return lax.dynamic_slice_in_dim(block, index * size, size, axis=axis)


def gathered(kept, came, weights_of):
    core, member, groups = (lax.axis_index("lon"), lax.axis_index("member"), lax.axis_size("lev"))
    halves = [jnp.concatenate([*half], axis=2) for half in (kept[2:], came[2:], kept[:2], came[:2])]
    rows = jnp.concatenate([jnp.stack(halves[:2]), crossed(jnp.stack(halves[2:]), "member")])
    pieces = lax.all_to_all(rows, "lev", split_axis=3, concat_axis=0, tiled=True)
    count, share, tiles, height, _ = pieces.shape
    values = pieces.transpose(0, 1, 3, 2, 4).reshape(count * share, height, tiles * LANES)
    matrix = packing(tiles * LANES, 2 * tiles, core, 0).astype(jnp.float32)
    values = jnp.einsum("mrp,pc->mrc", values, matrix, precision=lax.Precision.HIGHEST)
    weights = weights_of(
        [(g, m, c) for g in range(groups) for m in (member, 1 - member) for c in (core, 1 - core)]
    )
    return jnp.einsum("lm,mrc->lrc", weights, values, precision=lax.Precision.HIGHEST)


def per_device(land_mask, diffusivity, balance, member_id, counter_key):
    levels, height, breadth = land_mask.shape
    members, cores, groups, strips = (lax.axis_size(a) for a in ("member", "lon", "lev", "lat"))
    core, member, group = (lax.axis_index(a) for a in ("lon", "member", "lev"))
    assert members == 2 and cores == 2 and height > SWEEPS
    halo = SWEEPS
    pitch = (height + 2 * halo) // SUB
    share = -(-levels // 4)
    spare = share * 4 - levels
    if spare:
        land_mask, diffusivity = (jnp.pad(v, ((0, spare), (0, 0), (0, 0))) for v in (land_mask, diffusivity))
    mine, send, top, top_cross, bottom, bottom_cross = packed_conduct(halo, share, land_mask, diffusivity)
    ids = jnp.concatenate([counter_key, member_id])
    other_ids = crossed(ids, "member")
    top, other_ids = lax.optimization_barrier((top, other_ids))
    top, bottom = shifted(top, 1, False), shifted(bottom, -1, False)
    top_cross, bottom_cross = shifted(top_cross, 1, True), shifted(bottom_cross, -1, True)
    theirs = crossed(send, "lon")
    tiles = breadth * cores // LANES
    sizes = (levels, halo, (share, tiles, pitch, SUB, LANES), height * strips, breadth * cores)
    source = noise(other_ids, ids, *sizes)
    *kept, sent = diffuse(halo, groups == 2, mine, theirs, top, top_cross, bottom, bottom_cross, source)

    def weights_of(order):
        padded = jnp.pad(balance.reshape(-1, groups, levels), ((0, 0), (0, 0), (0, spare)))
        padded = padded.reshape(-1, groups * 4 * share)
        return jnp.concatenate([part(padded, g * 4 + m * 2 + c, share, 1) for g, m, c in order], axis=1)

    came = crossed(sent, "lon")
    if groups != 2:
        return gathered(kept, came, weights_of)
    other_near, other_far, near, far = (jnp.stack([a, b]) for a, b in zip(kept, came))
    diagonal = crossed(other_far, "member", "lev")
    along_x = crossed(far, "lev")
    along_y = crossed(other_near, "member")
    places = [(group, member), (group, 1 - member), (1 - group, 1 - member), (1 - group, member)]
    weights = weights_of([(g, m, c) for g, m in places for c in (core, 1 - core)])
    near = unpacked((near, along_y))
    return balanced(weights, near, (diagonal, along_x))


def solution(mesh):
    in_specs = (P("lev", "lat", "lon"), P("lev", "lat", "lon"), P(), P("member"), P("member"))
    out_specs = P("member", ("lat", "lev"), "lon")
    return jax.shard_map(
        per_device, mesh=mesh, in_specs=in_specs, out_specs=out_specs, check_vma=False
    )
```

```python
import functools
import math

import jax
import jax.numpy as jnp
from jax import lax
from jax.experimental import pallas as pl
from jax.experimental.pallas import tpu as pltpu
from jax.sharding import PartitionSpec as P

SWEEPS = 12
SOME = 3
noise_scale = math.sqrt(3.0) / 65536.0
LANES, SUB = 128, 8
HALF = LANES // 2
VMEM = pltpu.VMEM
whole = functools.partial(pl.BlockSpec, memory_space=pltpu.VMEM)
scalars = functools.partial(pl.BlockSpec, memory_space=pltpu.SMEM)


def budget(mebibytes):
    return pltpu.CompilerParams(vmem_limit_bytes=mebibytes << 20)


def scramble(values):
    values = values * 1103515245 + 12345
    values = values ^ (values >> 15)
    values = values * 747796405 + 1013904223
    values = values ^ (values >> 13)
    values = values * 277803737
    return values ^ (values >> 16)


def draw(index, stream_base):
    first = scramble(index ^ stream_base)
    second = scramble(first + 1664525)
    total = (
        (first & 65535)
        + ((first >> 16) & 65535)
        + (second & 65535)
        + ((second >> 16) & 65535)
        - 131070
    )
    return total.astype(jnp.float32) * noise_scale


def packed_source(columns, tiles, core):
    lane = columns & (LANES - 1)
    tile = (columns // LANES) + (tiles // 2) * ((lane // HALF) ^ core)
    return (lane & (HALF - 1)) * tiles + tile


def packing(width, tiles, core, axis):
    natural = lax.broadcasted_iota(jnp.int32, (width, width), 1 - axis)
    columns = lax.broadcasted_iota(jnp.int32, (width, width), axis)
    return jnp.where(packed_source(columns, tiles, core) == natural, 1.0, 0.0).astype(jnp.bfloat16)


def split(values):
    high = values.astype(jnp.bfloat16)
    return high, (values - high.astype(jnp.float32)).astype(jnp.bfloat16)


def permuted(values, matrix):
    rows = values.shape[0]
    both = jnp.dot(jnp.concatenate(split(values), axis=0), matrix, preferred_element_type=jnp.float32)
    return both[:rows] + both[rows:]


def edge_rows(some, pairs, halo):
    return -(-some * pairs * halo // SUB) * SUB


def conduct_kernel(halo, some, kept, other, mine, send, mine_edges, send_edges, matrix):
    levels, height, width = kept.shape
    pairs = width // LANES
    matrix[...] = packing(width, 2 * pairs, lax.axis_index("lon"), 1)
    for source, rows, edges in ((other, send, send_edges), (kept, mine, mine_edges)):
        moved = permuted(source[...].reshape(levels * height, width), matrix[...])
        for l in range(levels):
            for v in range(pairs):
                value = moved[l * height : (l + 1) * height, v * LANES : (v + 1) * LANES]
                rows[l, v] = value
                edge = pl.ds((l % some * pairs + v) * halo, halo)
                edges[0, l // some, edge, :] = value[height - halo :]
                edges[1, l // some, edge, :] = value[:halo]


def packed_conduct(halo, kept, other):
    share, height, width = kept.shape
    some, pairs = math.gcd(share, SOME), width // LANES
    rows = jax.ShapeDtypeStruct((share, pairs, height, LANES), jnp.float32)
    edge = jax.ShapeDtypeStruct((2, share // some, edge_rows(some, pairs, halo), LANES), jnp.float32)
    return pl.pallas_call(
        functools.partial(conduct_kernel, halo, some),
        out_shape=(rows, rows, edge, edge),
        in_specs=[whole()] * 2,
        out_specs=(whole(),) * 4,
        scratch_shapes=[VMEM((width, width), jnp.bfloat16)],
        compiler_params=budget(8),
    )(kept, other)


def noise_kernel(levels_here, halo, total_rows, total_cols, other, own, out):
    _, levels, tiles, pitch = out.shape[:4]
    quarter = lax.axis_index("member") * 2 + lax.axis_index("lon")
    level0 = lax.axis_index("lev") * levels_here + quarter * levels
    row0 = lax.axis_index("lat") * (total_rows // lax.axis_size("lat")) - halo
    sub = lax.broadcasted_iota(jnp.int32, (SUB, LANES), 0)
    lane = lax.broadcasted_iota(jnp.int32, (SUB, LANES), 1)
    within = sub * (pitch * total_cols) + lane * tiles
    bases = [other[...], own[...]]

    @pl.loop(0, levels)
    def _(l):
        start = ((level0 + l) * total_rows + row0) * total_cols
        for i, base in enumerate(bases):
            for t in range(tiles):
                for k in range(pitch):
                    out[i, l, t, k] = draw(within + (start + k * total_cols + t), base)


def noise(other, own, levels_here, halo, shape, total_rows, total_cols):
    return pl.pallas_call(
        functools.partial(noise_kernel, levels_here, halo, total_rows, total_cols),
        out_shape=jax.ShapeDtypeStruct((2, *shape), jnp.float32),
        in_specs=[whole()] * 2,
        out_specs=whole(),
        compiler_params=budget(8),
    )(other, own)


def neighbour_sums(old, tiles, pitch, emit):
    some = range(old.shape[0])
    first = [[old[g, t, 0] for t in range(tiles)] for g in some]
    last = [[old[g, t, pitch - 1] for t in range(tiles)] for g in some]
    above = [[pltpu.roll(v, 1, 0) for v in last[g]] for g in some]
    here = first
    for k in range(pitch):
        if k == pitch - 1:
            below = [[pltpu.roll(v, SUB - 1, 0) for v in first[g]] for g in some]
        elif k == pitch - 2:
            below = last
        else:
            below = [[old[g, t, k + 1] for t in range(tiles)] for g in some]
        for g in some:
            row = here[g]
            west = [pltpu.roll(row[-1], 1, 1)] + row[:-1]
            east = row[1:] + [pltpu.roll(row[0], LANES - 1, 1)]
            for t in ORDER(tiles):
                emit(g, t, k, row[t], (west[t] + east[t]) + (above[g][t] + below[g][t]))
        above, here = here, below


def ORDER(tiles):
    return [*range(1, tiles - 1), 0, tiles - 1]


def diffuse_kernel(halo, halves, mine, theirs, top, bottom, source, *refs):
    *kept, sent, rows, cond, gain, push, inv, u0, u1, res = refs
    _, levels, tiles, pitch = source.shape[:4]
    pairs, height = mine.shape[1], mine.shape[2]
    final = height // 2
    core = lax.axis_index("lon")
    group = lax.axis_index("lev") if halves else 0
    some = cond.shape[0]

    def on_left(shape):
        lane = lax.broadcasted_iota(jnp.int32, shape, len(shape) - 1)
        return (lane // HALF) == core

    def sweep(old, new):
        def step(g, t, k, value, total):
            new[g, t, k] = push[g, t, k] + gain[g % some, t, k] * total

        neighbour_sums(old, tiles, pitch, step)

    @pl.loop(0, levels // some)
    def _(block):
        for g in range(some):
            l = block * some + g
            for v in range(pairs):
                edge = pl.ds((g * pairs + v) * halo, halo)
                for p, q, start in (
                    (top[0, block, edge, :], top[1, block, edge, :], 0),
                    (mine[l, v], theirs[l, v], halo),
                    (bottom[0, block, edge, :], bottom[1, block, edge, :], halo + height),
                ):
                    count = p.shape[0]
                    left = on_left(p.shape)
                    rows[g, v, pl.ds(start, count), :] = jnp.where(left, p, q)
                    rows[g, v + pairs, pl.ds(start, count), :] = pltpu.roll(jnp.where(left, q, p), HALF, 1)
            for t in range(tiles):
                for k in range(pitch):
                    cond[g, t, k] = rows[g, t, pl.ds(k, SUB, stride=pitch), :]

        def prepare(g, t, k, c, total):
            r = 1.0 / (1.0 + c * total)
            q = c * r
            inv[g, t, k] = r
            gain[g, t, k] = q * c
            for i in range(2):
                s = source[i, block * some + g, t, k]
                push[i * some + g, t, k] = q * s
                u0[i * some + g, t, k] = c * s

        neighbour_sums(cond, tiles, pitch, prepare)

        @pl.loop(0, (SWEEPS - 2) // 2)
        def _(i):
            sweep(u0, u1)
            sweep(u1, u0)

        sweep(u0, u1)

        def finish(g, t, k, value, total):
            i, g = divmod(g, some)
            c, s = cond[g, t, k], source[i, block * some + g, t, k]
            value = jnp.where(c != 0.0, (s + c * total) * inv[g, t, k], 0.0)
            res[i * some + g, t, pl.ds(k, SUB, stride=pitch), :] = value

        neighbour_sums(u1, tiles, pitch, finish)
        left = on_left((height, LANES))
        first = group == 0
        for i in range(2):
            for g in range(some):
                l = block * some + g
                for v in range(pairs):
                    a = res[i * some + g, v, pl.ds(halo, height), :]
                    b = pltpu.roll(res[i * some + g, v + pairs, pl.ds(halo, height), :], HALF, 1)
                    keep, send = jnp.where(left, a, b), jnp.where(left, b, a)
                    for value, close, away in (
                        (keep, kept[2 * i], kept[2 * i + 1]), (send, sent.at[2 * i], sent.at[2 * i + 1]),
                    ):
                        upper, lower = value[:final], value[final:]
                        close[l, v] = jnp.where(first, upper, lower)
                        away[l, v] = jnp.where(first, lower, upper)


def diffuse(halo, halves, *operands):
    levels, pairs, height, _ = operands[0].shape
    tiles, pitch = operands[-1].shape[2:4]
    some = math.gcd(levels, SOME)
    tile = VMEM((some, tiles, pitch, SUB, LANES), jnp.float32)
    both = VMEM((2 * some, tiles, pitch, SUB, LANES), jnp.float32)
    line = VMEM((2 * some, tiles, pitch * SUB, LANES), jnp.float32)
    result = jax.ShapeDtypeStruct((levels, pairs, height // 2, LANES), jnp.float32)
    return pl.pallas_call(
        functools.partial(diffuse_kernel, halo, halves),
        out_shape=(result,) * 4 + (jax.ShapeDtypeStruct((4, *result.shape), jnp.float32),),
        in_specs=[whole()] * len(operands),
        out_specs=(whole(),) * 5,
        scratch_shapes=[line, tile, tile, both, tile, both, both, line],
        compiler_params=budget(18),
    )(*operands)


def unpack(pieces, matrix, out, start):
    for piece in (p.at[i] for p in pieces for i in range(2)):
        levels, tiles, height, _ = piece.shape
        values = jnp.concatenate(
            [piece[:, t].reshape(levels * height, LANES) for t in range(tiles)], axis=1
        )
        moved = permuted(values, matrix)
        for t in range(tiles):
            out[start : start + levels, t] = moved[:, t * LANES : (t + 1) * LANES].reshape(levels, height, LANES)
        start += levels


def unpack_kernel(*refs):
    *pieces, out = refs
    tiles = pieces[0].shape[2]
    unpack(pieces, packing(tiles * LANES, 2 * tiles, lax.axis_index("lon"), 0), out, 0)


def unpacked(pieces):
    _, levels, tiles, height, _ = pieces[0].shape
    return pl.pallas_call(
        unpack_kernel,
        out_shape=jax.ShapeDtypeStruct((2 * len(pieces) * levels, tiles, height, LANES), jnp.float32),
        in_specs=[whole()] * len(pieces),
        out_specs=whole(),
        compiler_params=budget(8),
    )(*pieces)


def balance_kernel(weights, near, *refs):
    *pieces, out, columns, result = refs
    total = weights.shape[0]
    count, tiles, height, _ = columns.shape
    pitch = tiles * height
    columns[: near.shape[0]] = near[...]
    unpack(pieces, packing(tiles * LANES, 2 * tiles, lax.axis_index("lon"), 0), columns, near.shape[0])
    flat = columns.reshape(count * pitch, LANES)
    high, low = split(weights[...])
    stacked = jnp.concatenate([high, high, low], axis=1)
    for r in range(height):
        for t in range(tiles):
            top, rest = split(flat[pl.ds(t * height + r, count, stride=pitch), :])
            right = jnp.concatenate([top, rest, top], axis=0)
            result[pl.ds(t * height + r, total, stride=pitch), :] = jnp.dot(
                stacked, right, preferred_element_type=jnp.float32
            )
    for t in range(tiles):
        for l in range(total):
            start = l * pitch + t * height
            out[l, :, t * LANES : (t + 1) * LANES] = result[start : start + height, :]


def balanced(weights, near, pieces):
    _, tiles, height, _ = near.shape
    total, count = weights.shape
    return pl.pallas_call(
        balance_kernel,
        out_shape=jax.ShapeDtypeStruct((total, height, tiles * LANES), jnp.float32),
        in_specs=[whole()] * (2 + len(pieces)),
        out_specs=whole(),
        scratch_shapes=[
            VMEM((count, tiles, height, LANES), jnp.float32),
            VMEM((total * tiles * height, LANES), jnp.float32),
        ],
        compiler_params=budget(12),
    )(weights, near, *pieces)


def crossed(block, *axes):
    count = math.prod(lax.axis_size(a) for a in axes)
    return lax.ppermute(block, axes, [(i, count - 1 - i) for i in range(count)])


def shifted(block, step):
    strips = lax.axis_size("lat")
    return lax.ppermute(block, "lat", [(i, i + step) for i in range(strips) if 0 <= i + step < strips])


def part(block, index, size, axis):
    return lax.dynamic_slice_in_dim(block, index * size, size, axis=axis)


def gathered(kept, came, weights_of):
    core, member, groups = (lax.axis_index("lon"), lax.axis_index("member"), lax.axis_size("lev"))
    halves = [jnp.concatenate([*half], axis=2) for half in (kept[2:], came[2:], kept[:2], came[:2])]
    rows = jnp.concatenate([jnp.stack(halves[:2]), crossed(jnp.stack(halves[2:]), "member")])
    pieces = lax.all_to_all(rows, "lev", split_axis=3, concat_axis=0, tiled=True)
    count, share, tiles, height, _ = pieces.shape
    values = pieces.transpose(0, 1, 3, 2, 4).reshape(count * share, height, tiles * LANES)
    matrix = packing(tiles * LANES, 2 * tiles, core, 0).astype(jnp.float32)
    values = jnp.einsum("mrp,pc->mrc", values, matrix, precision=lax.Precision.HIGHEST)
    weights = weights_of(
        [(g, m, c) for g in range(groups) for m in (member, 1 - member) for c in (core, 1 - core)]
    )
    return jnp.einsum("lm,mrc->lrc", weights, values, precision=lax.Precision.HIGHEST)


def per_device(land_mask, diffusivity, balance, member_id, counter_key):
    levels, height, breadth = land_mask.shape
    members, cores, groups, strips = (lax.axis_size(a) for a in ("member", "lon", "lev", "lat"))
    core, member, group = (lax.axis_index(a) for a in ("lon", "member", "lev"))
    assert members == 2 and cores == 2 and height > SWEEPS
    halo = SWEEPS
    pitch = (height + 2 * halo) // SUB
    share = -(-levels // 4)
    spare = share * 4 - levels
    if spare:
        land_mask, diffusivity = (jnp.pad(v, ((0, spare), (0, 0), (0, 0))) for v in (land_mask, diffusivity))
    kept, other = (
        part(diffusivity, member * 2 + c, share, 0) * part(land_mask, member * 2 + c, share, 0).astype(jnp.float32)
        for c in (core, 1 - core)
    )
    mine, send, mine_edges, send_edges = packed_conduct(halo, kept, other)
    edges = jnp.stack([mine_edges, crossed(send_edges, "lon")], axis=1)
    theirs = crossed(send, "lon")
    top, bottom = shifted(edges[0], 1), shifted(edges[1], -1)
    base = jnp.broadcast_to(counter_key[0] * 69069 + member_id[0] * 362437, (SUB, LANES))
    other_base = crossed(base, "member")
    tiles = breadth * cores // LANES
    sizes = (levels, halo, (share, tiles, pitch, SUB, LANES), height * strips, breadth * cores)
    source = noise(other_base, base, *sizes)
    *kept, sent = diffuse(halo, groups == 2, mine, theirs, top, bottom, source)

    def weights_of(order):
        padded = jnp.pad(balance.reshape(-1, groups, levels), ((0, 0), (0, 0), (0, spare)))
        padded = padded.reshape(-1, groups * 4 * share)
        return jnp.concatenate([part(padded, g * 4 + m * 2 + c, share, 1) for g, m, c in order], axis=1)

    came = crossed(sent, "lon")
    if groups != 2:
        return gathered(kept, came, weights_of)
    other_near, other_far, near, far = (jnp.stack([a, b]) for a, b in zip(kept, came))
    diagonal = crossed(other_far, "member", "lev")
    along_x = crossed(far, "lev")
    along_y = crossed(other_near, "member")
    places = [(group, member), (group, 1 - member), (1 - group, 1 - member), (1 - group, member)]
    weights = weights_of([(g, m, c) for g, m in places for c in (core, 1 - core)])
    near = unpacked((near, along_y))
    return balanced(weights, near, (diagonal, along_x))


def solution(mesh):
    in_specs = (P("lev", "lat", "lon"), P("lev", "lat", "lon"), P(), P("member"), P("member"))
    out_specs = P("member", ("lat", "lev"), "lon")
    return jax.shard_map(
        per_device, mesh=mesh, in_specs=in_specs, out_specs=out_specs, check_vma=False
    )
```

```python
import functools
import math

import jax
import jax.numpy as jnp
from jax import lax
from jax.experimental import pallas as pl
from jax.experimental.pallas import tpu as pltpu
from jax.sharding import PartitionSpec as P

SWEEPS = 12
SOME = 3
noise_scale = math.sqrt(3.0) / 65536.0
LANES, SUB = 128, 8
HALF = LANES // 2
VMEM = pltpu.VMEM
whole = functools.partial(pl.BlockSpec, memory_space=pltpu.VMEM)
scalars = functools.partial(pl.BlockSpec, memory_space=pltpu.SMEM)


def budget(mebibytes):
    return pltpu.CompilerParams(vmem_limit_bytes=mebibytes << 20)


def scramble(values):
    values = values * 1103515245 + 12345
    values = values ^ (values >> 15)
    values = values * 747796405 + 1013904223
    values = values ^ (values >> 13)
    values = values * 277803737
    return values ^ (values >> 16)


def draw(index, stream_base):
    first = scramble(index ^ stream_base)
    second = scramble(first + 1664525)
    total = (
        (first & 65535)
        + ((first >> 16) & 65535)
        + (second & 65535)
        + ((second >> 16) & 65535)
        - 131070
    )
    return total.astype(jnp.float32) * noise_scale


def packed_source(columns, tiles, core):
    lane = columns & (LANES - 1)
    tile = (columns // LANES) + (tiles // 2) * ((lane // HALF) ^ core)
    return (lane & (HALF - 1)) * tiles + tile


def packing(width, tiles, core, axis):
    natural = lax.broadcasted_iota(jnp.int32, (width, width), 1 - axis)
    columns = lax.broadcasted_iota(jnp.int32, (width, width), axis)
    return jnp.where(packed_source(columns, tiles, core) == natural, 1.0, 0.0).astype(jnp.bfloat16)


def split(values):
    high = values.astype(jnp.bfloat16)
    return high, (values - high.astype(jnp.float32)).astype(jnp.bfloat16)


def permuted(values, matrix):
    rows = values.shape[0]
    both = jnp.dot(jnp.concatenate(split(values), axis=0), matrix, preferred_element_type=jnp.float32)
    return both[:rows] + both[rows:]


def edge_rows(some, pairs, halo):
    return -(-some * pairs * halo // SUB) * SUB


def conduct_kernel(halo, some, kept, other, mine, send, mine_edges, send_edges, matrix):
    levels, height, width = kept.shape
    pairs = width // LANES
    matrix[...] = packing(width, 2 * pairs, lax.axis_index("lon"), 1)
    for source, rows, edges in ((other, send, send_edges), (kept, mine, mine_edges)):
        moved = permuted(source[...].reshape(levels * height, width), matrix[...])
        for l in range(levels):
            for v in range(pairs):
                value = moved[l * height : (l + 1) * height, v * LANES : (v + 1) * LANES]
                rows[l, v] = value
                edge = pl.ds((l % some * pairs + v) * halo, halo)
                edges[0, l // some, edge, :] = value[height - halo :]
                edges[1, l // some, edge, :] = value[:halo]


def packed_conduct(halo, kept, other):
    share, height, width = kept.shape
    some, pairs = math.gcd(share, SOME), width // LANES
    rows = jax.ShapeDtypeStruct((share, pairs, height, LANES), jnp.float32)
    edge = jax.ShapeDtypeStruct((2, share // some, edge_rows(some, pairs, halo), LANES), jnp.float32)
    return pl.pallas_call(
        functools.partial(conduct_kernel, halo, some),
        out_shape=(rows, rows, edge, edge),
        in_specs=[whole()] * 2,
        out_specs=(whole(),) * 4,
        scratch_shapes=[VMEM((width, width), jnp.bfloat16)],
        compiler_params=budget(8),
    )(kept, other)


def noise_kernel(levels_here, halo, total_rows, total_cols, base, out):
    levels, tiles, pitch = out.shape[:3]
    quarter = lax.axis_index("member") * 2 + lax.axis_index("lon")
    level0 = lax.axis_index("lev") * levels_here + quarter * levels
    row0 = lax.axis_index("lat") * (total_rows // lax.axis_size("lat")) - halo
    sub = lax.broadcasted_iota(jnp.int32, (SUB, LANES), 0)
    lane = lax.broadcasted_iota(jnp.int32, (SUB, LANES), 1)
    within = sub * (pitch * total_cols) + lane * tiles
    stream = base[...]

    @pl.loop(0, levels)
    def _(l):
        start = ((level0 + l) * total_rows + row0) * total_cols
        for t in range(tiles):
            for k in range(pitch):
                out[l, t, k] = draw(within + (start + k * total_cols + t), stream)


def noise(base, levels_here, halo, shape, total_rows, total_cols):
    return pl.pallas_call(
        functools.partial(noise_kernel, levels_here, halo, total_rows, total_cols),
        out_shape=jax.ShapeDtypeStruct(shape, jnp.float32),
        in_specs=[whole()],
        out_specs=whole(),
        compiler_params=budget(8),
    )(base)


def neighbour_sums(old, tiles, pitch, emit):
    some = range(old.shape[0])
    first = [[old[g, t, 0] for t in range(tiles)] for g in some]
    last = [[old[g, t, pitch - 1] for t in range(tiles)] for g in some]
    above = [[pltpu.roll(v, 1, 0) for v in last[g]] for g in some]
    here = first
    for k in range(pitch):
        if k == pitch - 1:
            below = [[pltpu.roll(v, SUB - 1, 0) for v in first[g]] for g in some]
        elif k == pitch - 2:
            below = last
        else:
            below = [[old[g, t, k + 1] for t in range(tiles)] for g in some]
        for g in some:
            row = here[g]
            west = [pltpu.roll(row[-1], 1, 1)] + row[:-1]
            east = row[1:] + [pltpu.roll(row[0], LANES - 1, 1)]
            for t in ORDER(tiles):
                emit(g, t, k, row[t], (west[t] + east[t]) + (above[g][t] + below[g][t]))
        above, here = here, below


def ORDER(tiles):
    return [*range(1, tiles - 1), 0, tiles - 1]


def diffuse_kernel(halo, halves, start_block, mine, theirs, top, bottom, other_source, own_source, *refs):
    *kept, sent, rows, cond, gain, push, inv, u0, u1, res = refs
    sources = (other_source, own_source)
    tiles, pitch = own_source.shape[1:3]
    pairs, height = mine.shape[1], mine.shape[2]
    final = height // 2
    core = lax.axis_index("lon")
    group = lax.axis_index("lev") if halves else 0
    some = cond.shape[0]

    def on_left(shape):
        lane = lax.broadcasted_iota(jnp.int32, shape, len(shape) - 1)
        return (lane // HALF) == core

    def sweep(old, new):
        def step(g, t, k, value, total):
            new[g, t, k] = push[g, t, k] + gain[g % some, t, k] * total

        neighbour_sums(old, tiles, pitch, step)

    @pl.loop(start_block, start_block + kept[0].shape[0] // some)
    def _(block):
        for g in range(some):
            l = block * some + g
            for v in range(pairs):
                edge = pl.ds((g * pairs + v) * halo, halo)
                for p, q, start in (
                    (top[0, block, edge, :], top[1, block, edge, :], 0),
                    (mine[l, v], theirs[l, v], halo),
                    (bottom[0, block, edge, :], bottom[1, block, edge, :], halo + height),
                ):
                    count = p.shape[0]
                    left = on_left(p.shape)
                    rows[g, v, pl.ds(start, count), :] = jnp.where(left, p, q)
                    rows[g, v + pairs, pl.ds(start, count), :] = pltpu.roll(jnp.where(left, q, p), HALF, 1)
            for t in range(tiles):
                for k in range(pitch):
                    cond[g, t, k] = rows[g, t, pl.ds(k, SUB, stride=pitch), :]

        def prepare(g, t, k, c, total):
            r = 1.0 / (1.0 + c * total)
            q = c * r
            inv[g, t, k] = r
            gain[g, t, k] = q * c
            for i in range(2):
                s = sources[i][block * some + g, t, k]
                push[i * some + g, t, k] = q * s
                u0[i * some + g, t, k] = c * s

        neighbour_sums(cond, tiles, pitch, prepare)

        @pl.loop(0, (SWEEPS - 2) // 2)
        def _(i):
            sweep(u0, u1)
            sweep(u1, u0)

        sweep(u0, u1)

        def finish(g, t, k, value, total):
            i, g = divmod(g, some)
            c, s = cond[g, t, k], sources[i][block * some + g, t, k]
            value = jnp.where(c != 0.0, (s + c * total) * inv[g, t, k], 0.0)
            res[i * some + g, t, pl.ds(k, SUB, stride=pitch), :] = value

        neighbour_sums(u1, tiles, pitch, finish)
        left = on_left((height, LANES))
        first = group == 0
        for i in range(2):
            for g in range(some):
                l = (block - start_block) * some + g
                for v in range(pairs):
                    a = res[i * some + g, v, pl.ds(halo, height), :]
                    b = pltpu.roll(res[i * some + g, v + pairs, pl.ds(halo, height), :], HALF, 1)
                    keep, send = jnp.where(left, a, b), jnp.where(left, b, a)
                    for value, close, away in (
                        (keep, kept[2 * i], kept[2 * i + 1]), (send, sent.at[2 * i], sent.at[2 * i + 1]),
                    ):
                        upper, lower = value[:final], value[final:]
                        close[l, v] = jnp.where(first, upper, lower)
                        away[l, v] = jnp.where(first, lower, upper)


def diffuse(halo, halves, blocks, *operands):
    levels, pairs, height, _ = operands[0].shape
    tiles, pitch = operands[-1].shape[1:3]
    some = math.gcd(levels, SOME)
    tile = VMEM((some, tiles, pitch, SUB, LANES), jnp.float32)
    both = VMEM((2 * some, tiles, pitch, SUB, LANES), jnp.float32)
    line = VMEM((2 * some, tiles, pitch * SUB, LANES), jnp.float32)
    result = jax.ShapeDtypeStruct((len(blocks) * some, pairs, height // 2, LANES), jnp.float32)
    return pl.pallas_call(
        functools.partial(diffuse_kernel, halo, halves, blocks[0]),
        out_shape=(result,) * 4 + (jax.ShapeDtypeStruct((4, *result.shape), jnp.float32),),
        in_specs=[whole()] * len(operands),
        out_specs=(whole(),) * 5,
        scratch_shapes=[line, tile, tile, both, tile, both, both, line],
        compiler_params=budget(18),
    )(*operands)


def unpack(pieces, matrix, out):
    start = 0
    for piece in (p.at[i] for p in pieces for i in range(2)):
        levels, tiles, height, _ = piece.shape
        values = jnp.concatenate(
            [piece[:, t].reshape(levels * height, LANES) for t in range(tiles)], axis=1
        )
        moved = permuted(values, matrix)
        for t in range(tiles):
            out[start : start + levels, t] = moved[:, t * LANES : (t + 1) * LANES].reshape(levels, height, LANES)
        start += levels


def chosen(balance, places, width):
    total = balance.shape[1]
    core, member, group = (lax.axis_index(a) for a in ("lon", "member", "lev"))
    column = lax.broadcasted_iota(jnp.int32, (total, width), 1)
    level, offset = jnp.full((total, width), -1, jnp.int32), 0
    share = total // 8
    for across, swapped, start, size in places:
        for c in (core, 1 - core):
            g = 1 - group if across else group
            m = 1 - member if swapped else member
            first = (g * 4 + m * 2 + c) * share + start - offset
            level = jnp.where((column >= offset) & (column < offset + size), column + first, level)
            offset += size
    select = jnp.where(lax.broadcasted_iota(jnp.int32, (total, width), 0) == level, 1.0, 0.0).astype(jnp.bfloat16)
    high, low = (
        jnp.dot(v, select, preferred_element_type=jnp.float32).astype(jnp.bfloat16) for v in split(balance[...])
    )
    return jnp.concatenate([high, high, low], axis=1)


def weighted(balance, places, pieces, columns, emit):
    total = balance.shape[0]
    count, tiles, height, _ = columns.shape
    pitch = tiles * height
    unpack(pieces, packing(tiles * LANES, 2 * tiles, lax.axis_index("lon"), 0), columns)
    flat = columns.reshape(count * pitch, LANES)
    stacked = chosen(balance, places, count)
    for t in range(tiles):
        for r in range(height):
            top, rest = split(flat[pl.ds(t * height + r, count, stride=pitch), :])
            right = jnp.concatenate([top, rest, top], axis=0)
            value = jnp.dot(stacked, right, preferred_element_type=jnp.float32)
            emit(t, r, pl.ds(t * height + r, total, stride=pitch), value)


def early_kernel(places, weights, *refs):
    *pieces, out, columns = refs

    def store(t, r, rows, value):
        out[rows, :] = value

    weighted(weights, places, pieces, columns, store)


def late_kernel(places, weights, early, *refs):
    *pieces, out, columns, result, sent = refs
    total = weights.shape[0]
    tiles, height = columns.shape[1:3]
    copies = []

    def store(t, r, rows, value):
        result[rows, :] = early[rows, :] + value
        if r == height - 1:
            copy = pltpu.make_async_copy(
                result.reshape(total, tiles, height, LANES).at[:, t],
                out.at[:, :, pl.ds(t * LANES, LANES)],
                sent.at[t],
            )
            copy.start()
            copies.append(copy)

    weighted(weights, places, pieces, columns, store)
    for copy in copies:
        copy.wait()


def balanced(weights, places, pieces, early=None):
    total, count = weights.shape[0], sum(2 * p.shape[1] for p in pieces)
    tiles, height = pieces[0].shape[2:4]
    flat = (total * tiles * height, LANES)
    columns = VMEM((count, tiles, height, LANES), jnp.float32)
    if early is None:
        return pl.pallas_call(
            functools.partial(early_kernel, places),
            out_shape=jax.ShapeDtypeStruct(flat, jnp.float32),
            in_specs=[whole()] * (1 + len(pieces)),
            out_specs=whole(),
            scratch_shapes=[columns],
            compiler_params=budget(10),
        )(weights, *pieces)
    return pl.pallas_call(
        functools.partial(late_kernel, places),
        out_shape=jax.ShapeDtypeStruct((total, height, tiles * LANES), jnp.float32),
        in_specs=[whole()] * (2 + len(pieces)),
        out_specs=pl.BlockSpec(memory_space=pl.ANY),
        scratch_shapes=[columns, VMEM(flat, jnp.float32), pltpu.SemaphoreType.DMA((tiles,))],
        compiler_params=budget(10),
    )(weights, early, *pieces)


def crossed(block, *axes):
    count = math.prod(lax.axis_size(a) for a in axes)
    return lax.ppermute(block, axes, [(i, count - 1 - i) for i in range(count)])


def shifted(block, step):
    strips = lax.axis_size("lat")
    return lax.ppermute(block, "lat", [(i, i + step) for i in range(strips) if 0 <= i + step < strips])


def part(block, index, size, axis):
    return lax.dynamic_slice_in_dim(block, index * size, size, axis=axis)


def gathered(kept, came, balance, levels):
    core, member, groups = (lax.axis_index("lon"), lax.axis_index("member"), lax.axis_size("lev"))
    halves = [jnp.concatenate([*half], axis=2) for half in (kept[2:], came[2:], kept[:2], came[:2])]
    rows = jnp.concatenate([jnp.stack(halves[:2]), crossed(jnp.stack(halves[2:]), "member")])
    pieces = lax.all_to_all(rows, "lev", split_axis=3, concat_axis=0, tiled=True)
    count, share, tiles, height, _ = pieces.shape
    values = pieces.transpose(0, 1, 3, 2, 4).reshape(count * share, height, tiles * LANES)
    matrix = packing(tiles * LANES, 2 * tiles, core, 0).astype(jnp.float32)
    values = jnp.einsum("mrp,pc->mrc", values, matrix, precision=lax.Precision.HIGHEST)
    spare = 4 * share - levels
    padded = jnp.pad(balance.reshape(-1, groups, levels), ((0, 0), (0, 0), (0, spare)))
    padded = padded.reshape(-1, groups * 4 * share)
    order = [(g, m, c) for g in range(groups) for m in (member, 1 - member) for c in (core, 1 - core)]
    weights = jnp.concatenate([part(padded, g * 4 + m * 2 + c, share, 1) for g, m, c in order], axis=1)
    return jnp.einsum("lm,mrc->lrc", weights, values, precision=lax.Precision.HIGHEST)


def per_device(land_mask, diffusivity, balance, member_id, counter_key):
    levels, height, breadth = land_mask.shape
    members, cores, groups, strips = (lax.axis_size(a) for a in ("member", "lon", "lev", "lat"))
    core, member, group = (lax.axis_index(a) for a in ("lon", "member", "lev"))
    assert members == 2 and cores == 2 and height > SWEEPS
    halo = SWEEPS
    pitch = (height + 2 * halo) // SUB
    share = -(-levels // 4)
    spare = share * 4 - levels
    if spare:
        land_mask, diffusivity = (jnp.pad(v, ((0, spare), (0, 0), (0, 0))) for v in (land_mask, diffusivity))
    kept, other = (
        part(diffusivity, member * 2 + c, share, 0) * part(land_mask, member * 2 + c, share, 0).astype(jnp.float32)
        for c in (core, 1 - core)
    )
    mine, send, mine_edges, send_edges = packed_conduct(halo, kept, other)
    edges = jnp.stack([mine_edges, crossed(send_edges, "lon")], axis=1)
    theirs = crossed(send, "lon")
    top, bottom = shifted(edges[0], 1), shifted(edges[1], -1)
    base = jnp.broadcast_to(counter_key[0] * 69069 + member_id[0] * 362437, (SUB, LANES))
    other_base = crossed(base, "member")
    tiles = breadth * cores // LANES
    sizes = (levels, halo, (share, tiles, pitch, SUB, LANES), height * strips, breadth * cores)
    own_source = noise(base, *sizes)
    other_source = noise(other_base, *sizes)
    blocks = range(share // math.gcd(share, SOME))
    operands = (mine, theirs, top, bottom, other_source, own_source)

    if groups != 2:
        *kept, sent = diffuse(halo, False, blocks, *operands)
        return gathered(kept, crossed(sent, "lon"), balance, levels)
    cut = max(1, len(blocks) * 3 // 3)
    parts, start = {}, 0
    for i, some_blocks in enumerate(filter(len, (blocks[:cut], blocks[cut:]))):
        *kept, sent = diffuse(halo, True, some_blocks, *operands)
        came = crossed(sent, "lon")
        other_near, other_far, near, far = (jnp.stack([a, b]) for a, b in zip(kept, came))
        size = near.shape[1]
        parts["near", i] = near, (False, False, start, size)
        parts["diagonal", i] = crossed(other_far, "member", "lev"), (True, True, start, size)
        parts["x", i] = crossed(far, "lev"), (True, False, start, size)
        parts["y", i] = crossed(other_near, "member"), (False, True, start, size)
        start += size
    late = [parts[name, max(i for _, i in parts)] for name in ("x", "y")]
    soon = [p for p in parts.values() if all(p is not q for q in late)]
    pieces, places = zip(*soon)
    early = balanced(balance, places, pieces)
    pieces, places = zip(*late)
    return balanced(balance, places, pieces, early)


def solution(mesh):
    in_specs = (P("lev", "lat", "lon"), P("lev", "lat", "lon"), P(), P("member"), P("member"))
    out_specs = P("member", ("lat", "lev"), "lon")
    return jax.shard_map(
        per_device, mesh=mesh, in_specs=in_specs, out_specs=out_specs, check_vma=False
    )
```

```python
import functools
import math

import jax
import jax.numpy as jnp
from jax import lax
from jax.experimental import pallas as pl
from jax.experimental.pallas import tpu as pltpu
from jax.sharding import PartitionSpec as P

SWEEPS = 12
SOME = 3
noise_scale = math.sqrt(3.0) / 65536.0
LANES, SUB = 128, 8
HALF = LANES // 2
VMEM = pltpu.VMEM
whole = functools.partial(pl.BlockSpec, memory_space=pltpu.VMEM)
scalars = functools.partial(pl.BlockSpec, memory_space=pltpu.SMEM)


def budget(mebibytes):
    return pltpu.CompilerParams(vmem_limit_bytes=mebibytes << 20)


def scramble(values):
    values = values * 1103515245 + 12345
    values = values ^ (values >> 15)
    values = values * 747796405 + 1013904223
    values = values ^ (values >> 13)
    values = values * 277803737
    return values ^ (values >> 16)


def draw(index, stream_base):
    first = scramble(index ^ stream_base)
    second = scramble(first + 1664525)
    total = (
        (first & 65535)
        + ((first >> 16) & 65535)
        + (second & 65535)
        + ((second >> 16) & 65535)
        - 131070
    )
    return total.astype(jnp.float32) * noise_scale


def packed_source(columns, tiles, core):
    lane = columns & (LANES - 1)
    tile = (columns // LANES) + (tiles // 2) * ((lane // HALF) ^ core)
    return (lane & (HALF - 1)) * tiles + tile


def packing(width, tiles, core, axis):
    natural = lax.broadcasted_iota(jnp.int32, (width, width), 1 - axis)
    columns = lax.broadcasted_iota(jnp.int32, (width, width), axis)
    return jnp.where(packed_source(columns, tiles, core) == natural, 1.0, 0.0).astype(jnp.bfloat16)


def split(values):
    high = values.astype(jnp.bfloat16)
    return high, (values - high.astype(jnp.float32)).astype(jnp.bfloat16)


def permuted(values, matrix):
    rows = values.shape[0]
    both = jnp.dot(jnp.concatenate(split(values), axis=0), matrix, preferred_element_type=jnp.float32)
    return both[:rows] + both[rows:]


def edge_rows(some, pairs, halo):
    return -(-some * pairs * halo // SUB) * SUB


def conduct_kernel(halo, some, kept, other, mine, send, mine_edges, send_edges, matrix):
    levels, height, width = kept.shape
    pairs = width // LANES
    matrix[...] = packing(width, 2 * pairs, lax.axis_index("lon"), 1)
    for source, rows, edges in ((other, send, send_edges), (kept, mine, mine_edges)):
        moved = permuted(source[...].reshape(levels * height, width), matrix[...])
        for l in range(levels):
            for v in range(pairs):
                value = moved[l * height : (l + 1) * height, v * LANES : (v + 1) * LANES]
                rows[l, v] = value
                edge = pl.ds((l % some * pairs + v) * halo, halo)
                edges[0, l // some, edge, :] = value[height - halo :]
                edges[1, l // some, edge, :] = value[:halo]


def packed_conduct(halo, kept, other):
    share, height, width = kept.shape
    some, pairs = math.gcd(share, SOME), width // LANES
    rows = jax.ShapeDtypeStruct((share, pairs, height, LANES), jnp.float32)
    edge = jax.ShapeDtypeStruct((2, share // some, edge_rows(some, pairs, halo), LANES), jnp.float32)
    return pl.pallas_call(
        functools.partial(conduct_kernel, halo, some),
        out_shape=(rows, rows, edge, edge),
        in_specs=[whole()] * 2,
        out_specs=(whole(),) * 4,
        scratch_shapes=[VMEM((width, width), jnp.bfloat16)],
        compiler_params=budget(8),
    )(kept, other)


def noise_kernel(levels_here, halo, total_rows, total_cols, base, out):
    levels, tiles, pitch = out.shape[:3]
    quarter = lax.axis_index("member") * 2 + lax.axis_index("lon")
    level0 = lax.axis_index("lev") * levels_here + quarter * levels
    row0 = lax.axis_index("lat") * (total_rows // lax.axis_size("lat")) - halo
    sub = lax.broadcasted_iota(jnp.int32, (SUB, LANES), 0)
    lane = lax.broadcasted_iota(jnp.int32, (SUB, LANES), 1)
    within = sub * (pitch * total_cols) + lane * tiles
    stream = base[...]

    @pl.loop(0, levels)
    def _(l):
        start = ((level0 + l) * total_rows + row0) * total_cols
        for t in range(tiles):
            for k in range(pitch):
                out[l, t, k] = draw(within + (start + k * total_cols + t), stream)


def noise(base, levels_here, halo, shape, total_rows, total_cols):
    return pl.pallas_call(
        functools.partial(noise_kernel, levels_here, halo, total_rows, total_cols),
        out_shape=jax.ShapeDtypeStruct(shape, jnp.float32),
        in_specs=[whole()],
        out_specs=whole(),
        compiler_params=budget(8),
    )(base)


def neighbour_sums(old, tiles, pitch, emit):
    some = range(old.shape[0])

    def row(g, k):
        values = [old[g, t, k] for t in range(tiles)]
        return [pltpu.roll(values[-1], 1, 1), *values, pltpu.roll(values[0], LANES - 1, 1)]

    first = [row(g, 0) for g in some]
    above = [[pltpu.roll(old[g, t, pitch - 1], 1, 0) for t in range(tiles)] for g in some]
    pairs = [[above[g][t] + first[g][t] for t in range(tiles)] for g in some]
    here = first
    for k in range(pitch):
        if k == pitch - 1:
            below = [[None, *(pltpu.roll(v, SUB - 1, 0) for v in first[g][1:-1]), None] for g in some]
        else:
            below = [row(g, k + 1) for g in some]
        for g in some:
            now, later = here[g], below[g]
            fresh = [None if t == 0 and later[0] is None else now[t + 1] + later[t] for t in range(tiles + 1)]
            for t in range(tiles):
                emit(g, t, k, now[t + 1], fresh[t + 1] + pairs[g][t])
            pairs[g] = fresh
        here = below


def diffuse_kernel(halo, halves, start_block, mine, theirs, top, bottom, other_source, own_source, *refs):
    *kept, sent, rows, cond, gain, push, inv, u0, u1, res = refs
    sources = (other_source, own_source)
    tiles, pitch = own_source.shape[1:3]
    pairs, height = mine.shape[1], mine.shape[2]
    final = height // 2
    core = lax.axis_index("lon")
    group = lax.axis_index("lev") if halves else 0
    some = cond.shape[0]

    def on_left(shape):
        lane = lax.broadcasted_iota(jnp.int32, shape, len(shape) - 1)
        return (lane // HALF) == core

    def sweep(old, new):
        def step(g, t, k, value, total):
            new[g, t, k] = push[g, t, k] + gain[g % some, t, k] * total

        neighbour_sums(old, tiles, pitch, step)

    @pl.loop(start_block, start_block + kept[0].shape[0] // some)
    def _(block):
        for g in range(some):
            l = block * some + g
            for v in range(pairs):
                edge = pl.ds((g * pairs + v) * halo, halo)
                for p, q, start in (
                    (top[0, block, edge, :], top[1, block, edge, :], 0),
                    (mine[l, v], theirs[l, v], halo),
                    (bottom[0, block, edge, :], bottom[1, block, edge, :], halo + height),
                ):
                    count = p.shape[0]
                    left = on_left(p.shape)
                    rows[g, v, pl.ds(start, count), :] = jnp.where(left, p, q)
                    rows[g, v + pairs, pl.ds(start, count), :] = pltpu.roll(jnp.where(left, q, p), HALF, 1)
            for t in range(tiles):
                for k in range(pitch):
                    cond[g, t, k] = rows[g, t, pl.ds(k, SUB, stride=pitch), :]

        def prepare(g, t, k, c, total):
            r = 1.0 / (1.0 + c * total)
            q = c * r
            inv[g, t, k] = r
            gain[g, t, k] = q * c
            for i in range(2):
                s = sources[i][block * some + g, t, k]
                push[i * some + g, t, k] = q * s
                u0[i * some + g, t, k] = c * s

        neighbour_sums(cond, tiles, pitch, prepare)

        for i in range(SWEEPS - 1):
            sweep(*((u0, u1) if i % 2 == 0 else (u1, u0)))

        def finish(g, t, k, value, total):
            i, g = divmod(g, some)
            c, s = cond[g, t, k], sources[i][block * some + g, t, k]
            value = jnp.where(c != 0.0, (s + c * total) * inv[g, t, k], 0.0)
            res[i * some + g, t, pl.ds(k, SUB, stride=pitch), :] = value

        neighbour_sums(u1, tiles, pitch, finish)
        left = on_left((height, LANES))
        first = group == 0
        for i in range(2):
            for g in range(some):
                l = (block - start_block) * some + g
                for v in range(pairs):
                    a = res[i * some + g, v, pl.ds(halo, height), :]
                    b = pltpu.roll(res[i * some + g, v + pairs, pl.ds(halo, height), :], HALF, 1)
                    keep, send = jnp.where(left, a, b), jnp.where(left, b, a)
                    for value, close, away in (
                        (keep, kept[2 * i], kept[2 * i + 1]), (send, sent.at[2 * i], sent.at[2 * i + 1]),
                    ):
                        upper, lower = value[:final], value[final:]
                        close[l, v] = jnp.where(first, upper, lower)
                        away[l, v] = jnp.where(first, lower, upper)


def diffuse(halo, halves, blocks, *operands):
    levels, pairs, height, _ = operands[0].shape
    tiles, pitch = operands[-1].shape[1:3]
    some = math.gcd(levels, SOME)
    tile = VMEM((some, tiles, pitch, SUB, LANES), jnp.float32)
    both = VMEM((2 * some, tiles, pitch, SUB, LANES), jnp.float32)
    line = VMEM((2 * some, tiles, pitch * SUB, LANES), jnp.float32)
    result = jax.ShapeDtypeStruct((len(blocks) * some, pairs, height // 2, LANES), jnp.float32)
    return pl.pallas_call(
        functools.partial(diffuse_kernel, halo, halves, blocks[0]),
        out_shape=(result,) * 4 + (jax.ShapeDtypeStruct((4, *result.shape), jnp.float32),),
        in_specs=[whole()] * len(operands),
        out_specs=(whole(),) * 5,
        scratch_shapes=[line, tile, tile, both, tile, both, both, line],
        compiler_params=budget(18),
    )(*operands)


def unpack(pieces, matrix, out):
    start = 0
    for piece in (p.at[i] for p in pieces for i in range(2)):
        levels, tiles, height, _ = piece.shape
        values = jnp.concatenate(
            [piece[:, t].reshape(levels * height, LANES) for t in range(tiles)], axis=1
        )
        moved = permuted(values, matrix)
        for t in range(tiles):
            out[start : start + levels, t] = moved[:, t * LANES : (t + 1) * LANES].reshape(levels, height, LANES)
        start += levels


def chosen(balance, places, width):
    total = balance.shape[1]
    core, member, group = (lax.axis_index(a) for a in ("lon", "member", "lev"))
    column = lax.broadcasted_iota(jnp.int32, (total, width), 1)
    level, offset = jnp.full((total, width), -1, jnp.int32), 0
    share = total // 8
    for across, swapped, start, size in places:
        for c in (core, 1 - core):
            g = 1 - group if across else group
            m = 1 - member if swapped else member
            first = (g * 4 + m * 2 + c) * share + start - offset
            level = jnp.where((column >= offset) & (column < offset + size), column + first, level)
            offset += size
    select = jnp.where(lax.broadcasted_iota(jnp.int32, (total, width), 0) == level, 1.0, 0.0).astype(jnp.bfloat16)
    high, low = (
        jnp.dot(v, select, preferred_element_type=jnp.float32).astype(jnp.bfloat16) for v in split(balance[...])
    )
    return jnp.concatenate([high, high, low], axis=1)


def weighted(balance, places, pieces, columns, emit):
    total = balance.shape[0]
    count, tiles, height, _ = columns.shape
    pitch = tiles * height
    unpack(pieces, packing(tiles * LANES, 2 * tiles, lax.axis_index("lon"), 0), columns)
    flat = columns.reshape(count * pitch, LANES)
    stacked = chosen(balance, places, count)
    for t in range(tiles):
        for r in range(height):
            top, rest = split(flat[pl.ds(t * height + r, count, stride=pitch), :])
            right = jnp.concatenate([top, rest, top], axis=0)
            value = jnp.dot(stacked, right, preferred_element_type=jnp.float32)
            emit(t, r, pl.ds(t * height + r, total, stride=pitch), value)


def early_kernel(places, weights, *refs):
    *pieces, out, columns = refs

    def store(t, r, rows, value):
        out[rows, :] = value

    weighted(weights, places, pieces, columns, store)


def late_kernel(places, weights, early, *refs):
    *pieces, out, columns, result, sent = refs
    total = weights.shape[0]
    tiles, height = columns.shape[1:3]
    copies = []

    def store(t, r, rows, value):
        result[rows, :] = early[rows, :] + value
        if r == height - 1:
            copy = pltpu.make_async_copy(
                result.reshape(total, tiles, height, LANES).at[:, t],
                out.at[:, :, pl.ds(t * LANES, LANES)],
                sent.at[t],
            )
            copy.start()
            copies.append(copy)

    weighted(weights, places, pieces, columns, store)
    for copy in copies:
        copy.wait()


def balanced(weights, places, pieces, early=None):
    total, count = weights.shape[0], sum(2 * p.shape[1] for p in pieces)
    tiles, height = pieces[0].shape[2:4]
    flat = (total * tiles * height, LANES)
    columns = VMEM((count, tiles, height, LANES), jnp.float32)
    if early is None:
        return pl.pallas_call(
            functools.partial(early_kernel, places),
            out_shape=jax.ShapeDtypeStruct(flat, jnp.float32),
            in_specs=[whole()] * (1 + len(pieces)),
            out_specs=whole(),
            scratch_shapes=[columns],
            compiler_params=budget(10),
        )(weights, *pieces)
    return pl.pallas_call(
        functools.partial(late_kernel, places),
        out_shape=jax.ShapeDtypeStruct((total, height, tiles * LANES), jnp.float32),
        in_specs=[whole()] * (2 + len(pieces)),
        out_specs=pl.BlockSpec(memory_space=pl.ANY),
        scratch_shapes=[columns, VMEM(flat, jnp.float32), pltpu.SemaphoreType.DMA((tiles,))],
        compiler_params=budget(10),
    )(weights, early, *pieces)


def crossed(block, *axes):
    count = math.prod(lax.axis_size(a) for a in axes)
    return lax.ppermute(block, axes, [(i, count - 1 - i) for i in range(count)])


def shifted(block, step):
    strips = lax.axis_size("lat")
    return lax.ppermute(block, "lat", [(i, i + step) for i in range(strips) if 0 <= i + step < strips])


def part(block, index, size, axis):
    return lax.dynamic_slice_in_dim(block, index * size, size, axis=axis)


def gathered(kept, came, balance, levels):
    core, member, groups = (lax.axis_index("lon"), lax.axis_index("member"), lax.axis_size("lev"))
    halves = [jnp.concatenate([*half], axis=2) for half in (kept[2:], came[2:], kept[:2], came[:2])]
    rows = jnp.concatenate([jnp.stack(halves[:2]), crossed(jnp.stack(halves[2:]), "member")])
    pieces = lax.all_to_all(rows, "lev", split_axis=3, concat_axis=0, tiled=True)
    count, share, tiles, height, _ = pieces.shape
    values = pieces.transpose(0, 1, 3, 2, 4).reshape(count * share, height, tiles * LANES)
    matrix = packing(tiles * LANES, 2 * tiles, core, 0).astype(jnp.float32)
    values = jnp.einsum("mrp,pc->mrc", values, matrix, precision=lax.Precision.HIGHEST)
    spare = 4 * share - levels
    padded = jnp.pad(balance.reshape(-1, groups, levels), ((0, 0), (0, 0), (0, spare)))
    padded = padded.reshape(-1, groups * 4 * share)
    order = [(g, m, c) for g in range(groups) for m in (member, 1 - member) for c in (core, 1 - core)]
    weights = jnp.concatenate([part(padded, g * 4 + m * 2 + c, share, 1) for g, m, c in order], axis=1)
    return jnp.einsum("lm,mrc->lrc", weights, values, precision=lax.Precision.HIGHEST)


def per_device(land_mask, diffusivity, balance, member_id, counter_key):
    levels, height, breadth = land_mask.shape
    members, cores, groups, strips = (lax.axis_size(a) for a in ("member", "lon", "lev", "lat"))
    core, member, group = (lax.axis_index(a) for a in ("lon", "member", "lev"))
    assert members == 2 and cores == 2 and height > SWEEPS
    halo = SWEEPS
    pitch = (height + 2 * halo) // SUB
    share = -(-levels // 4)
    spare = share * 4 - levels
    if spare:
        land_mask, diffusivity = (jnp.pad(v, ((0, spare), (0, 0), (0, 0))) for v in (land_mask, diffusivity))
    kept, other = (
        part(diffusivity, member * 2 + c, share, 0) * part(land_mask, member * 2 + c, share, 0).astype(jnp.float32)
        for c in (core, 1 - core)
    )
    mine, send, mine_edges, send_edges = packed_conduct(halo, kept, other)
    edges = jnp.stack([mine_edges, crossed(send_edges, "lon")], axis=1)
    theirs = crossed(send, "lon")
    top, bottom = shifted(edges[0], 1), shifted(edges[1], -1)
    base = jnp.broadcast_to(counter_key[0] * 69069 + member_id[0] * 362437, (SUB, LANES))
    other_base = crossed(base, "member")
    tiles = breadth * cores // LANES
    sizes = (levels, halo, (share, tiles, pitch, SUB, LANES), height * strips, breadth * cores)
    own_source = noise(base, *sizes)
    other_source = noise(other_base, *sizes)
    blocks = range(share // math.gcd(share, SOME))
    operands = (mine, theirs, top, bottom, other_source, own_source)

    if groups != 2:
        *kept, sent = diffuse(halo, False, blocks, *operands)
        return gathered(kept, crossed(sent, "lon"), balance, levels)
    cut = max(1, len(blocks) * 3 // 3)
    parts, start = {}, 0
    for i, some_blocks in enumerate(filter(len, (blocks[:cut], blocks[cut:]))):
        *kept, sent = diffuse(halo, True, some_blocks, *operands)
        came = crossed(sent, "lon")
        other_near, other_far, near, far = (jnp.stack([a, b]) for a, b in zip(kept, came))
        size = near.shape[1]
        parts["near", i] = near, (False, False, start, size)
        parts["diagonal", i] = crossed(other_far, "member", "lev"), (True, True, start, size)
        parts["x", i] = crossed(far, "lev"), (True, False, start, size)
        parts["y", i] = crossed(other_near, "member"), (False, True, start, size)
        start += size
    late = [parts[name, max(i for _, i in parts)] for name in ("x", "y")]
    soon = [p for p in parts.values() if all(p is not q for q in late)]
    pieces, places = zip(*soon)
    early = balanced(balance, places, pieces)
    pieces, places = zip(*late)
    return balanced(balance, places, pieces, early)


def solution(mesh):
    in_specs = (P("lev", "lat", "lon"), P("lev", "lat", "lon"), P(), P("member"), P("member"))
    out_specs = P("member", ("lat", "lev"), "lon")
    return jax.shard_map(
        per_device, mesh=mesh, in_specs=in_specs, out_specs=out_specs, check_vma=False
    )
```

```python
import functools
import math

import jax
import jax.numpy as jnp
from jax import lax
from jax.experimental import pallas as pl
from jax.experimental.pallas import tpu as pltpu
from jax.sharding import PartitionSpec as P

SWEEPS = 12
SOME = 3
noise_scale = math.sqrt(3.0) / 65536.0
LANES, SUB = 128, 8
HALF = LANES // 2
VMEM = pltpu.VMEM
whole = functools.partial(pl.BlockSpec, memory_space=pltpu.VMEM)
scalars = functools.partial(pl.BlockSpec, memory_space=pltpu.SMEM)


def budget(mebibytes):
    return pltpu.CompilerParams(vmem_limit_bytes=mebibytes << 20)


def scramble(values):
    values = values * 1103515245 + 12345
    values = values ^ (values >> 15)
    values = values * 747796405 + 1013904223
    values = values ^ (values >> 13)
    values = values * 277803737
    return values ^ (values >> 16)


def draw(index, stream_base):
    first = scramble(index ^ stream_base)
    second = scramble(first + 1664525)
    total = (
        (first & 65535)
        + ((first >> 16) & 65535)
        + (second & 65535)
        + ((second >> 16) & 65535)
        - 131070
    )
    return total.astype(jnp.float32) * noise_scale


def packed_source(columns, tiles, core):
    lane = columns & (LANES - 1)
    tile = (columns // LANES) + (tiles // 2) * ((lane // HALF) ^ core)
    return (lane & (HALF - 1)) * tiles + tile


def packing(width, tiles, core, axis):
    natural = lax.broadcasted_iota(jnp.int32, (width, width), 1 - axis)
    columns = lax.broadcasted_iota(jnp.int32, (width, width), axis)
    return jnp.where(packed_source(columns, tiles, core) == natural, 1.0, 0.0).astype(jnp.bfloat16)


def split(values):
    high = values.astype(jnp.bfloat16)
    return high, (values - high.astype(jnp.float32)).astype(jnp.bfloat16)


def permuted(values, matrix):
    rows = values.shape[0]
    both = jnp.dot(jnp.concatenate(split(values), axis=0), matrix, preferred_element_type=jnp.float32)
    return both[:rows] + both[rows:]


def edge_rows(some, pairs, halo):
    return -(-some * pairs * halo // SUB) * SUB


def conduct_kernel(halo, some, kept, other, mine, send, mine_edges, send_edges, matrix):
    levels, height, width = kept.shape
    pairs = width // LANES
    matrix[...] = packing(width, 2 * pairs, lax.axis_index("lon"), 1)
    for source, rows, edges in ((other, send, send_edges), (kept, mine, mine_edges)):
        moved = permuted(source[...].reshape(levels * height, width), matrix[...])
        for l in range(levels):
            for v in range(pairs):
                value = moved[l * height : (l + 1) * height, v * LANES : (v + 1) * LANES]
                rows[l, v] = value
                edge = pl.ds((l % some * pairs + v) * halo, halo)
                edges[0, l // some, edge, :] = value[height - halo :]
                edges[1, l // some, edge, :] = value[:halo]


def packed_conduct(halo, kept, other):
    share, height, width = kept.shape
    some, pairs = math.gcd(share, SOME), width // LANES
    rows = jax.ShapeDtypeStruct((share, pairs, height, LANES), jnp.float32)
    edge = jax.ShapeDtypeStruct((2, share // some, edge_rows(some, pairs, halo), LANES), jnp.float32)
    return pl.pallas_call(
        functools.partial(conduct_kernel, halo, some),
        out_shape=(rows, rows, edge, edge),
        in_specs=[whole()] * 2,
        out_specs=(whole(),) * 4,
        scratch_shapes=[VMEM((width, width), jnp.bfloat16)],
        compiler_params=budget(8),
    )(kept, other)


def noise_kernel(levels_here, halo, total_rows, total_cols, base, out):
    levels, tiles, pitch = out.shape[:3]
    quarter = lax.axis_index("member") * 2 + lax.axis_index("lon")
    level0 = lax.axis_index("lev") * levels_here + quarter * levels
    row0 = lax.axis_index("lat") * (total_rows // lax.axis_size("lat")) - halo
    sub = lax.broadcasted_iota(jnp.int32, (SUB, LANES), 0)
    lane = lax.broadcasted_iota(jnp.int32, (SUB, LANES), 1)
    within = sub * (pitch * total_cols) + lane * tiles
    stream = base[...]

    @pl.loop(0, levels)
    def _(l):
        start = ((level0 + l) * total_rows + row0) * total_cols
        for t in range(tiles):
            for k in range(pitch):
                out[l, t, k] = draw(within + (start + k * total_cols + t), stream)


def noise(base, levels_here, halo, shape, total_rows, total_cols):
    return pl.pallas_call(
        functools.partial(noise_kernel, levels_here, halo, total_rows, total_cols),
        out_shape=jax.ShapeDtypeStruct(shape, jnp.float32),
        in_specs=[whole()],
        out_specs=whole(),
        compiler_params=budget(8),
    )(base)


def neighbour_sums(old, tiles, pitch, emit):
    some = range(old.shape[0])

    def row(g, k):
        values = [old[g, t, k] for t in range(tiles)]
        return [pltpu.roll(values[-1], 1, 1), *values, pltpu.roll(values[0], LANES - 1, 1)]

    first = [row(g, 0) for g in some]
    above = [[pltpu.roll(old[g, t, pitch - 1], 1, 0) for t in range(tiles)] for g in some]
    pairs = [[above[g][t] + first[g][t] for t in range(tiles)] for g in some]
    here = first
    for k in range(pitch):
        if k == pitch - 1:
            below = [[None, *(pltpu.roll(v, SUB - 1, 0) for v in first[g][1:-1]), None] for g in some]
        else:
            below = [row(g, k + 1) for g in some]
        for g in some:
            now, later = here[g], below[g]
            fresh = [None if t == 0 and later[0] is None else now[t + 1] + later[t] for t in range(tiles + 1)]
            for t in range(tiles):
                emit(g, t, k, now[t + 1], fresh[t + 1] + pairs[g][t])
            pairs[g] = fresh
        here = below


def diffuse_kernel(halo, halves, start_block, mine, theirs, top, bottom, other_source, own_source, *refs):
    kept, sent = refs[:4], refs[4:8]
    rows, cond, gain, push, inv, u0, u1, res = refs[8:]
    sources = (other_source, own_source)
    tiles, pitch = own_source.shape[1:3]
    pairs, height = mine.shape[1], mine.shape[2]
    final = height // 2
    core = lax.axis_index("lon")
    group = lax.axis_index("lev") if halves else 0
    some = cond.shape[0]

    def on_left(shape):
        lane = lax.broadcasted_iota(jnp.int32, shape, len(shape) - 1)
        return (lane // HALF) == core

    def sweep(old, new):
        def step(g, t, k, value, total):
            new[g, t, k] = push[g, t, k] + gain[g % some, t, k] * total

        neighbour_sums(old, tiles, pitch, step)

    @pl.loop(start_block, start_block + kept[0].shape[0] // some)
    def _(block):
        for g in range(some):
            l = block * some + g
            for v in range(pairs):
                edge = pl.ds((g * pairs + v) * halo, halo)
                for p, q, start in (
                    (top[0, block, edge, :], top[1, block, edge, :], 0),
                    (mine[l, v], theirs[l, v], halo),
                    (bottom[0, block, edge, :], bottom[1, block, edge, :], halo + height),
                ):
                    count = p.shape[0]
                    left = on_left(p.shape)
                    rows[g, v, pl.ds(start, count), :] = jnp.where(left, p, q)
                    rows[g, v + pairs, pl.ds(start, count), :] = pltpu.roll(jnp.where(left, q, p), HALF, 1)
            for t in range(tiles):
                for k in range(pitch):
                    cond[g, t, k] = rows[g, t, pl.ds(k, SUB, stride=pitch), :]

        def prepare(g, t, k, c, total):
            r = 1.0 / (1.0 + c * total)
            q = c * r
            inv[g, t, k] = r
            gain[g, t, k] = q * c
            for i in range(2):
                s = sources[i][block * some + g, t, k]
                push[i * some + g, t, k] = q * s
                u0[i * some + g, t, k] = c * s

        neighbour_sums(cond, tiles, pitch, prepare)

        for i in range(SWEEPS - 1):
            sweep(*((u0, u1) if i % 2 == 0 else (u1, u0)))

        def finish(g, t, k, value, total):
            i, g = divmod(g, some)
            c, s = cond[g, t, k], sources[i][block * some + g, t, k]
            value = jnp.where(c != 0.0, (s + c * total) * inv[g, t, k], 0.0)
            res[i * some + g, t, pl.ds(k, SUB, stride=pitch), :] = value

        neighbour_sums(u1, tiles, pitch, finish)
        left = on_left((height, LANES))
        first = group == 0
        for i in range(2):
            for g in range(some):
                l = (block - start_block) * some + g
                for v in range(pairs):
                    a = res[i * some + g, v, pl.ds(halo, height), :]
                    b = pltpu.roll(res[i * some + g, v + pairs, pl.ds(halo, height), :], HALF, 1)
                    keep, send = jnp.where(left, a, b), jnp.where(left, b, a)
                    for value, close, away in (
                        (keep, kept[2 * i], kept[2 * i + 1]), (send, sent[2 * i], sent[2 * i + 1]),
                    ):
                        upper, lower = value[:final], value[final:]
                        close[l, v] = jnp.where(first, upper, lower)
                        away[l, v] = jnp.where(first, lower, upper)


def diffuse(halo, halves, blocks, *operands):
    levels, pairs, height, _ = operands[0].shape
    tiles, pitch = operands[-1].shape[1:3]
    some = math.gcd(levels, SOME)
    tile = VMEM((some, tiles, pitch, SUB, LANES), jnp.float32)
    both = VMEM((2 * some, tiles, pitch, SUB, LANES), jnp.float32)
    line = VMEM((2 * some, tiles, pitch * SUB, LANES), jnp.float32)
    result = jax.ShapeDtypeStruct((len(blocks) * some, pairs, height // 2, LANES), jnp.float32)
    return pl.pallas_call(
        functools.partial(diffuse_kernel, halo, halves, blocks[0]),
        out_shape=(result,) * 8,
        in_specs=[whole()] * len(operands),
        out_specs=(whole(),) * 8,
        scratch_shapes=[line, tile, tile, both, tile, both, both, line],
        compiler_params=budget(18),
    )(*operands)


def unpack(pieces, matrix, out):
    start = 0
    for piece in pieces:
        levels, tiles, height, _ = piece.shape
        values = jnp.concatenate(
            [piece[:, t].reshape(levels * height, LANES) for t in range(tiles)], axis=1
        )
        moved = permuted(values, matrix)
        for t in range(tiles):
            out[start : start + levels, t] = moved[:, t * LANES : (t + 1) * LANES].reshape(levels, height, LANES)
        start += levels


def chosen(balance, places, width):
    total = balance.shape[1]
    core, member, group = (lax.axis_index(a) for a in ("lon", "member", "lev"))
    column = lax.broadcasted_iota(jnp.int32, (total, width), 1)
    level, offset = jnp.full((total, width), -1, jnp.int32), 0
    share = total // 8
    for across, swapped, other in places:
        g = 1 - group if across else group
        m = 1 - member if swapped else member
        first = (g * 4 + m * 2 + (1 - core if other else core)) * share - offset
        level = jnp.where((column >= offset) & (column < offset + share), column + first, level)
        offset += share
    select = jnp.where(lax.broadcasted_iota(jnp.int32, (total, width), 0) == level, 1.0, 0.0).astype(jnp.bfloat16)
    high, low = (
        jnp.dot(v, select, preferred_element_type=jnp.float32).astype(jnp.bfloat16) for v in split(balance[...])
    )
    return jnp.concatenate([high, high, low], axis=1)


def weighted(balance, places, pieces, columns, emit):
    total = balance.shape[0]
    count, tiles, height, _ = columns.shape
    pitch = tiles * height
    unpack(pieces, packing(tiles * LANES, 2 * tiles, lax.axis_index("lon"), 0), columns)
    flat = columns.reshape(count * pitch, LANES)
    stacked = chosen(balance, places, count)
    for t in range(tiles):
        for r in range(height):
            top, rest = split(flat[pl.ds(t * height + r, count, stride=pitch), :])
            right = jnp.concatenate([top, rest, top], axis=0)
            value = jnp.dot(stacked, right, preferred_element_type=jnp.float32)
            emit(t, r, pl.ds(t * height + r, total, stride=pitch), value)


def early_kernel(places, weights, *refs):
    *pieces, out, columns = refs

    def store(t, r, rows, value):
        out[rows, :] = value

    weighted(weights, places, pieces, columns, store)


def late_kernel(places, weights, early, *refs):
    *pieces, out, columns, result, sent = refs
    total = weights.shape[0]
    tiles, height = columns.shape[1:3]
    copies = []

    def store(t, r, rows, value):
        result[rows, :] = early[rows, :] + value
        if r == height - 1:
            copy = pltpu.make_async_copy(
                result.reshape(total, tiles, height, LANES).at[:, t],
                out.at[:, :, pl.ds(t * LANES, LANES)],
                sent.at[t],
            )
            copy.start()
            copies.append(copy)

    weighted(weights, places, pieces, columns, store)
    for copy in copies:
        copy.wait()


def balanced(weights, places, pieces, early=None):
    total, count = weights.shape[0], sum(p.shape[0] for p in pieces)
    tiles, height = pieces[0].shape[1:3]
    flat = (total * tiles * height, LANES)
    columns = VMEM((count, tiles, height, LANES), jnp.float32)
    if early is None:
        return pl.pallas_call(
            functools.partial(early_kernel, places),
            out_shape=jax.ShapeDtypeStruct(flat, jnp.float32),
            in_specs=[whole()] * (1 + len(pieces)),
            out_specs=whole(),
            scratch_shapes=[columns],
            compiler_params=budget(10),
        )(weights, *pieces)
    return pl.pallas_call(
        functools.partial(late_kernel, places),
        out_shape=jax.ShapeDtypeStruct((total, height, tiles * LANES), jnp.float32),
        in_specs=[whole()] * (2 + len(pieces)),
        out_specs=pl.BlockSpec(memory_space=pl.ANY),
        scratch_shapes=[columns, VMEM(flat, jnp.float32), pltpu.SemaphoreType.DMA((tiles,))],
        compiler_params=budget(10),
    )(weights, early, *pieces)


def crossed(block, *axes):
    count = math.prod(lax.axis_size(a) for a in axes)
    return lax.ppermute(block, axes, [(i, count - 1 - i) for i in range(count)])


def shifted(block, step):
    strips = lax.axis_size("lat")
    return lax.ppermute(block, "lat", [(i, i + step) for i in range(strips) if 0 <= i + step < strips])


def part(block, index, size, axis):
    return lax.dynamic_slice_in_dim(block, index * size, size, axis=axis)


def gathered(kept, came, balance, levels):
    core, member, groups = (lax.axis_index("lon"), lax.axis_index("member"), lax.axis_size("lev"))
    halves = [jnp.concatenate([*half], axis=2) for half in (kept[2:], came[2:], kept[:2], came[:2])]
    rows = jnp.concatenate([jnp.stack(halves[:2]), crossed(jnp.stack(halves[2:]), "member")])
    pieces = lax.all_to_all(rows, "lev", split_axis=3, concat_axis=0, tiled=True)
    count, share, tiles, height, _ = pieces.shape
    values = pieces.transpose(0, 1, 3, 2, 4).reshape(count * share, height, tiles * LANES)
    matrix = packing(tiles * LANES, 2 * tiles, core, 0).astype(jnp.float32)
    values = jnp.einsum("mrp,pc->mrc", values, matrix, precision=lax.Precision.HIGHEST)
    spare = 4 * share - levels
    padded = jnp.pad(balance.reshape(-1, groups, levels), ((0, 0), (0, 0), (0, spare)))
    padded = padded.reshape(-1, groups * 4 * share)
    order = [(g, m, c) for g in range(groups) for m in (member, 1 - member) for c in (core, 1 - core)]
    weights = jnp.concatenate([part(padded, g * 4 + m * 2 + c, share, 1) for g, m, c in order], axis=1)
    return jnp.einsum("lm,mrc->lrc", weights, values, precision=lax.Precision.HIGHEST)


def per_device(land_mask, diffusivity, balance, member_id, counter_key):
    levels, height, breadth = land_mask.shape
    members, cores, groups, strips = (lax.axis_size(a) for a in ("member", "lon", "lev", "lat"))
    core, member, group = (lax.axis_index(a) for a in ("lon", "member", "lev"))
    assert members == 2 and cores == 2 and height > SWEEPS
    halo = SWEEPS
    pitch = (height + 2 * halo) // SUB
    share = -(-levels // 4)
    spare = share * 4 - levels
    if spare:
        land_mask, diffusivity = (jnp.pad(v, ((0, spare), (0, 0), (0, 0))) for v in (land_mask, diffusivity))
    kept, other = (
        part(diffusivity, member * 2 + c, share, 0) * part(land_mask, member * 2 + c, share, 0).astype(jnp.float32)
        for c in (core, 1 - core)
    )
    mine, send, mine_edges, send_edges = packed_conduct(halo, kept, other)
    edges = jnp.stack([mine_edges, crossed(send_edges, "lon")], axis=1)
    theirs = crossed(send, "lon")
    top, bottom = shifted(edges[0], 1), shifted(edges[1], -1)
    base = jnp.broadcast_to(counter_key[0] * 69069 + member_id[0] * 362437, (SUB, LANES))
    other_base = crossed(base, "member")
    tiles = breadth * cores // LANES
    sizes = (levels, halo, (share, tiles, pitch, SUB, LANES), height * strips, breadth * cores)
    own_source = noise(base, *sizes)
    other_source = noise(other_base, *sizes)
    blocks = range(share // math.gcd(share, SOME))
    operands = (mine, theirs, top, bottom, other_source, own_source)

    if groups != 2:
        outs = diffuse(halo, False, blocks, *operands)
        return gathered(outs[:4], crossed(jnp.stack(outs[4:]), "lon"), balance, levels)
    outs = diffuse(halo, True, blocks, *operands)
    other_near, other_far, near, far, other_near_send, other_far_send, near_send, far_send = outs
    diagonal = [crossed(other_far, "member", "lev"), crossed(other_far_send, "member", "lev", "lon")]
    along_x = [crossed(far, "lev"), crossed(far_send, "lev", "lon")]
    along_y = [crossed(other_near, "member"), crossed(other_near_send, "member", "lon")]
    here = [near, crossed(near_send, "lon")]

    def places(across, swapped):
        return [(across, swapped, other) for other in (False, True)]

    early = balanced(balance, places(False, False) + places(True, True), (*here, *diagonal))
    return balanced(balance, places(True, False) + places(False, True), (*along_x, *along_y), early)


def solution(mesh):
    in_specs = (P("lev", "lat", "lon"), P("lev", "lat", "lon"), P(), P("member"), P("member"))
    out_specs = P("member", ("lat", "lev"), "lon")
    return jax.shard_map(
        per_device, mesh=mesh, in_specs=in_specs, out_specs=out_specs, check_vma=False
    )
```

```python
import functools
import math

import jax
import jax.numpy as jnp
from jax import lax
from jax.experimental import pallas as pl
from jax.experimental.pallas import tpu as pltpu
from jax.sharding import PartitionSpec as P

SWEEPS = 12
SOME = 3
noise_scale = math.sqrt(3.0) / 65536.0
LANES, SUB = 128, 8
HALF = LANES // 2
VMEM = pltpu.VMEM
whole = functools.partial(pl.BlockSpec, memory_space=pltpu.VMEM)
scalars = functools.partial(pl.BlockSpec, memory_space=pltpu.SMEM)


def budget(mebibytes):
    return pltpu.CompilerParams(vmem_limit_bytes=mebibytes << 20)


def scramble(values):
    values = values * 1103515245 + 12345
    values = values ^ (values >> 15)
    values = values * 747796405 + 1013904223
    values = values ^ (values >> 13)
    values = values * 277803737
    return values ^ (values >> 16)


def draw(index, stream_base):
    first = scramble(index ^ stream_base)
    second = scramble(first + 1664525)
    total = (
        (first & 65535)
        + ((first >> 16) & 65535)
        + (second & 65535)
        + ((second >> 16) & 65535)
        - 131070
    )
    return total.astype(jnp.float32) * noise_scale


def packed_source(columns, tiles, core):
    lane = columns & (LANES - 1)
    tile = (columns // LANES) + (tiles // 2) * ((lane // HALF) ^ core)
    return (lane & (HALF - 1)) * tiles + tile


def packing(width, tiles, core, axis):
    natural = lax.broadcasted_iota(jnp.int32, (width, width), 1 - axis)
    columns = lax.broadcasted_iota(jnp.int32, (width, width), axis)
    return jnp.where(packed_source(columns, tiles, core) == natural, 1.0, 0.0).astype(jnp.bfloat16)


def split(values):
    high = values.astype(jnp.bfloat16)
    return high, (values - high.astype(jnp.float32)).astype(jnp.bfloat16)


def permuted(values, matrix):
    rows = values.shape[0]
    both = jnp.dot(jnp.concatenate(split(values), axis=0), matrix, preferred_element_type=jnp.float32)
    return both[:rows] + both[rows:]


def edge_rows(some, pairs, halo):
    return -(-some * pairs * halo // SUB) * SUB


def conduct_kernel(halo, some, kept, other, mine, send, mine_edges, send_edges, matrix):
    levels, height, width = kept.shape
    pairs = width // LANES
    matrix[...] = packing(width, 2 * pairs, lax.axis_index("lon"), 1)
    for source, rows, edges in ((other, send, send_edges), (kept, mine, mine_edges)):
        moved = permuted(source[...].reshape(levels * height, width), matrix[...])
        for l in range(levels):
            for v in range(pairs):
                value = moved[l * height : (l + 1) * height, v * LANES : (v + 1) * LANES]
                rows[l, v] = value
                edge = pl.ds((l % some * pairs + v) * halo, halo)
                edges[0, l // some, edge, :] = value[height - halo :]
                edges[1, l // some, edge, :] = value[:halo]


def packed_conduct(halo, kept, other):
    share, height, width = kept.shape
    some, pairs = math.gcd(share, SOME), width // LANES
    rows = jax.ShapeDtypeStruct((share, pairs, height, LANES), jnp.float32)
    edge = jax.ShapeDtypeStruct((2, share // some, edge_rows(some, pairs, halo), LANES), jnp.float32)
    return pl.pallas_call(
        functools.partial(conduct_kernel, halo, some),
        out_shape=(rows, rows, edge, edge),
        in_specs=[whole()] * 2,
        out_specs=(whole(),) * 4,
        scratch_shapes=[VMEM((width, width), jnp.bfloat16)],
        compiler_params=budget(8),
    )(kept, other)


def noise_kernel(levels_here, halo, total_rows, total_cols, base, out):
    levels, tiles, pitch = out.shape[:3]
    quarter = lax.axis_index("member") * 2 + lax.axis_index("lon")
    level0 = lax.axis_index("lev") * levels_here + quarter * levels
    row0 = lax.axis_index("lat") * (total_rows // lax.axis_size("lat")) - halo
    sub = lax.broadcasted_iota(jnp.int32, (SUB, LANES), 0)
    lane = lax.broadcasted_iota(jnp.int32, (SUB, LANES), 1)
    within = sub * (pitch * total_cols) + lane * tiles
    stream = base[...]

    @pl.loop(0, levels)
    def _(l):
        start = ((level0 + l) * total_rows + row0) * total_cols
        for t in range(tiles):
            for k in range(pitch):
                out[l, t, k] = draw(within + (start + k * total_cols + t), stream)


def noise(base, levels_here, halo, shape, total_rows, total_cols):
    return pl.pallas_call(
        functools.partial(noise_kernel, levels_here, halo, total_rows, total_cols),
        out_shape=jax.ShapeDtypeStruct(shape, jnp.float32),
        in_specs=[whole()],
        out_specs=whole(),
        compiler_params=budget(8),
    )(base)


def neighbour_sums(old, tiles, pitch, emit):
    some = range(old.shape[0])

    def row(g, k):
        values = [old[g, t, k] for t in range(tiles)]
        return [pltpu.roll(values[-1], 1, 1), *values, pltpu.roll(values[0], LANES - 1, 1)]

    first = [row(g, 0) for g in some]
    above = [[pltpu.roll(old[g, t, pitch - 1], 1, 0) for t in range(tiles)] for g in some]
    pairs = [[above[g][t] + first[g][t] for t in range(tiles)] for g in some]
    here = first
    for k in range(pitch):
        if k == pitch - 1:
            below = [[None, *(pltpu.roll(v, SUB - 1, 0) for v in first[g][1:-1]), None] for g in some]
        else:
            below = [row(g, k + 1) for g in some]
        for g in some:
            now, later = here[g], below[g]
            fresh = [None if t == 0 and later[0] is None else now[t + 1] + later[t] for t in range(tiles + 1)]
            for t in range(tiles):
                emit(g, t, k, now[t + 1], fresh[t + 1] + pairs[g][t])
            pairs[g] = fresh
        here = below


def diffuse_kernel(halo, halves, start_block, mine, theirs, top, bottom, other_source, own_source, *refs):
    kept, sent = refs[:4], refs[4:8]
    rows, cond, gain, push, inv, u0, u1, res = refs[8:]
    sources = (other_source, own_source)
    tiles, pitch = own_source.shape[1:3]
    pairs, height = mine.shape[1], mine.shape[2]
    final = height // 2
    core = lax.axis_index("lon")
    group = lax.axis_index("lev") if halves else 0
    some = cond.shape[0]

    def on_left(shape):
        lane = lax.broadcasted_iota(jnp.int32, shape, len(shape) - 1)
        return (lane // HALF) == core

    def sweep(old, new):
        def step(g, t, k, value, total):
            new[g, t, k] = push[g, t, k] + gain[g % some, t, k] * total

        neighbour_sums(old, tiles, pitch, step)

    @pl.loop(start_block, start_block + kept[0].shape[0] // some)
    def _(block):
        for g in range(some):
            l = block * some + g
            for v in range(pairs):
                edge = pl.ds((g * pairs + v) * halo, halo)
                for p, q, start in (
                    (top[0, block, edge, :], top[1, block, edge, :], 0),
                    (mine[l, v], theirs[l, v], halo),
                    (bottom[0, block, edge, :], bottom[1, block, edge, :], halo + height),
                ):
                    count = p.shape[0]
                    left = on_left(p.shape)
                    rows[g, v, pl.ds(start, count), :] = jnp.where(left, p, q)
                    rows[g, v + pairs, pl.ds(start, count), :] = pltpu.roll(jnp.where(left, q, p), HALF, 1)
            for t in range(tiles):
                for k in range(pitch):
                    cond[g, t, k] = rows[g, t, pl.ds(k, SUB, stride=pitch), :]

        def prepare(g, t, k, c, total):
            r = 1.0 / (1.0 + c * total)
            q = c * r
            inv[g, t, k] = r
            gain[g, t, k] = q * c
            for i in range(2):
                s = sources[i][block * some + g, t, k]
                push[i * some + g, t, k] = q * s
                u0[i * some + g, t, k] = c * s

        neighbour_sums(cond, tiles, pitch, prepare)

        for i in range(SWEEPS - 1):
            sweep(*((u0, u1) if i % 2 == 0 else (u1, u0)))

        def finish(g, t, k, value, total):
            i, g = divmod(g, some)
            c, s = cond[g, t, k], sources[i][block * some + g, t, k]
            value = jnp.where(c != 0.0, (s + c * total) * inv[g, t, k], 0.0)
            res[i * some + g, t, pl.ds(k, SUB, stride=pitch), :] = value

        neighbour_sums(u1, tiles, pitch, finish)
        left = on_left((height, LANES))
        first = group == 0
        for i in range(2):
            for g in range(some):
                l = (block - start_block) * some + g
                for v in range(pairs):
                    a = res[i * some + g, v, pl.ds(halo, height), :]
                    b = pltpu.roll(res[i * some + g, v + pairs, pl.ds(halo, height), :], HALF, 1)
                    keep, send = jnp.where(left, a, b), jnp.where(left, b, a)
                    for value, close, away in (
                        (keep, kept[2 * i], kept[2 * i + 1]), (send, sent[2 * i], sent[2 * i + 1]),
                    ):
                        upper, lower = value[:final], value[final:]
                        close[l, v] = jnp.where(first, upper, lower)
                        away[l, v] = jnp.where(first, lower, upper)


def diffuse(halo, halves, blocks, *operands):
    levels, pairs, height, _ = operands[0].shape
    tiles, pitch = operands[-1].shape[1:3]
    some = math.gcd(levels, SOME)
    tile = VMEM((some, tiles, pitch, SUB, LANES), jnp.float32)
    both = VMEM((2 * some, tiles, pitch, SUB, LANES), jnp.float32)
    line = VMEM((2 * some, tiles, (pitch + 1) * SUB, LANES), jnp.float32)
    result = jax.ShapeDtypeStruct((len(blocks) * some, pairs, height // 2, LANES), jnp.float32)
    return pl.pallas_call(
        functools.partial(diffuse_kernel, halo, halves, blocks[0]),
        out_shape=(result,) * 8,
        in_specs=[whole()] * len(operands),
        out_specs=(whole(),) * 8,
        scratch_shapes=[line, tile, tile, both, tile, both, both, line],
        compiler_params=budget(18),
    )(*operands)


def unpack(pieces, matrix, out):
    start = 0
    for piece in pieces:
        levels, tiles, height, _ = piece.shape
        values = jnp.concatenate(
            [piece[:, t].reshape(levels * height, LANES) for t in range(tiles)], axis=1
        )
        moved = permuted(values, matrix)
        for t in range(tiles):
            out[start : start + levels, t] = moved[:, t * LANES : (t + 1) * LANES].reshape(levels, height, LANES)
        start += levels


def chosen(balance, places, width):
    total = balance.shape[1]
    core, member, group = (lax.axis_index(a) for a in ("lon", "member", "lev"))
    column = lax.broadcasted_iota(jnp.int32, (total, width), 1)
    level, offset = jnp.full((total, width), -1, jnp.int32), 0
    share = total // 8
    for across, swapped, other in places:
        g = 1 - group if across else group
        m = 1 - member if swapped else member
        first = (g * 4 + m * 2 + (1 - core if other else core)) * share - offset
        level = jnp.where((column >= offset) & (column < offset + share), column + first, level)
        offset += share
    select = jnp.where(lax.broadcasted_iota(jnp.int32, (total, width), 0) == level, 1.0, 0.0).astype(jnp.bfloat16)
    high, low = (
        jnp.dot(v, select, preferred_element_type=jnp.float32).astype(jnp.bfloat16) for v in split(balance[...])
    )
    return jnp.concatenate([high, high, low], axis=1)


def weighted(balance, places, pieces, columns, emit):
    total = balance.shape[0]
    tiles, height = columns.shape[1:3]
    count, pitch = sum(p.shape[0] for p in pieces), tiles * height
    unpack(pieces, packing(tiles * LANES, 2 * tiles, lax.axis_index("lon"), 0), columns)
    flat = columns.reshape(columns.shape[0] * pitch, LANES)
    stacked = chosen(balance, places, count)
    for t in range(tiles):
        for r in range(height):
            top, rest = split(flat[pl.ds(t * height + r, count, stride=pitch), :])
            right = jnp.concatenate([top, rest, top], axis=0)
            value = jnp.dot(stacked, right, preferred_element_type=jnp.float32)
            emit(t, r, pl.ds(t * height + r, total, stride=pitch), value)


def share_kernel(places, weights, *refs):
    *pieces, out, columns = refs
    earlier = pieces.pop(0) if len(pieces) > len(places) else None

    def store(t, r, rows, value):
        out[rows, :] = value if earlier is None else earlier[rows, :] + value

    weighted(weights, places, pieces, columns, store)


def last_kernel(places, weights, earlier, *refs):
    *pieces, out, columns, result, sent = refs
    total = weights.shape[0]
    tiles, height = columns.shape[1:3]
    copies = []

    def store(t, r, rows, value):
        result[rows, :] = earlier[rows, :] + value
        if r % SUB == SUB - 1:
            some = pl.ds(r - SUB + 1, SUB)
            copy = pltpu.make_async_copy(
                result.reshape(total, tiles, height, LANES).at[:, t, some],
                out.at[:, some, pl.ds(t * LANES, LANES)],
                sent.at[t, r // SUB],
            )
            copy.start()
            copies.append(copy)

    weighted(weights, places, pieces, columns, store)
    for copy in copies:
        copy.wait()


def balanced(weights, places, pieces, earlier=None, last=False):
    total, count = weights.shape[0], sum(p.shape[0] for p in pieces)
    tiles, height = pieces[0].shape[1:3]
    flat = (total * tiles * height, LANES)
    columns = VMEM((-(-count // SUB) * SUB, tiles, height, LANES), jnp.float32)
    operands = (weights, *(() if earlier is None else (earlier,)), *pieces)
    if not last:
        return pl.pallas_call(
            functools.partial(share_kernel, places),
            out_shape=jax.ShapeDtypeStruct(flat, jnp.float32),
            in_specs=[whole()] * len(operands),
            out_specs=whole(),
            scratch_shapes=[columns],
            compiler_params=budget(10),
        )(*operands)
    return pl.pallas_call(
        functools.partial(last_kernel, places),
        out_shape=jax.ShapeDtypeStruct((total, height, tiles * LANES), jnp.float32),
        in_specs=[whole()] * len(operands),
        out_specs=pl.BlockSpec(memory_space=pl.ANY),
        scratch_shapes=[columns, VMEM(flat, jnp.float32), pltpu.SemaphoreType.DMA((tiles, height // SUB))],
        compiler_params=budget(10),
    )(*operands)


def crossed(block, *axes):
    count = math.prod(lax.axis_size(a) for a in axes)
    return lax.ppermute(block, axes, [(i, count - 1 - i) for i in range(count)])


def shifted(block, step):
    strips = lax.axis_size("lat")
    return lax.ppermute(block, "lat", [(i, i + step) for i in range(strips) if 0 <= i + step < strips])


def part(block, index, size, axis):
    return lax.dynamic_slice_in_dim(block, index * size, size, axis=axis)


def gathered(kept, came, balance, levels):
    core, member, groups = (lax.axis_index("lon"), lax.axis_index("member"), lax.axis_size("lev"))
    halves = [jnp.concatenate([*half], axis=2) for half in (kept[2:], came[2:], kept[:2], came[:2])]
    rows = jnp.concatenate([jnp.stack(halves[:2]), crossed(jnp.stack(halves[2:]), "member")])
    pieces = lax.all_to_all(rows, "lev", split_axis=3, concat_axis=0, tiled=True)
    count, share, tiles, height, _ = pieces.shape
    values = pieces.transpose(0, 1, 3, 2, 4).reshape(count * share, height, tiles * LANES)
    matrix = packing(tiles * LANES, 2 * tiles, core, 0).astype(jnp.float32)
    values = jnp.einsum("mrp,pc->mrc", values, matrix, precision=lax.Precision.HIGHEST)
    spare = 4 * share - levels
    padded = jnp.pad(balance.reshape(-1, groups, levels), ((0, 0), (0, 0), (0, spare)))
    padded = padded.reshape(-1, groups * 4 * share)
    order = [(g, m, c) for g in range(groups) for m in (member, 1 - member) for c in (core, 1 - core)]
    weights = jnp.concatenate([part(padded, g * 4 + m * 2 + c, share, 1) for g, m, c in order], axis=1)
    return jnp.einsum("lm,mrc->lrc", weights, values, precision=lax.Precision.HIGHEST)


def per_device(land_mask, diffusivity, balance, member_id, counter_key):
    levels, height, breadth = land_mask.shape
    members, cores, groups, strips = (lax.axis_size(a) for a in ("member", "lon", "lev", "lat"))
    core, member, group = (lax.axis_index(a) for a in ("lon", "member", "lev"))
    assert members == 2 and cores == 2 and height > SWEEPS
    halo = SWEEPS
    pitch = (height + 2 * halo) // SUB
    share = -(-levels // 4)
    spare = share * 4 - levels
    if spare:
        land_mask, diffusivity = (jnp.pad(v, ((0, spare), (0, 0), (0, 0))) for v in (land_mask, diffusivity))
    kept, other = (
        part(diffusivity, member * 2 + c, share, 0) * part(land_mask, member * 2 + c, share, 0).astype(jnp.float32)
        for c in (core, 1 - core)
    )
    mine, send, mine_edges, send_edges = packed_conduct(halo, kept, other)
    edges = jnp.stack([mine_edges, crossed(send_edges, "lon")], axis=1)
    theirs = crossed(send, "lon")
    top, bottom = shifted(edges[0], 1), shifted(edges[1], -1)
    base = jnp.broadcast_to(counter_key[0] * 69069 + member_id[0] * 362437, (SUB, LANES))
    other_base = crossed(base, "member")
    tiles = breadth * cores // LANES
    sizes = (levels, halo, (share, tiles, pitch, SUB, LANES), height * strips, breadth * cores)
    own_source = noise(base, *sizes)
    other_source = noise(other_base, *sizes)
    blocks = range(share // math.gcd(share, SOME))
    operands = (mine, theirs, top, bottom, other_source, own_source)

    if groups != 2:
        outs = diffuse(halo, False, blocks, *operands)
        return gathered(outs[:4], crossed(jnp.stack(outs[4:]), "lon"), balance, levels)
    outs = diffuse(halo, True, blocks, *operands)
    other_near, other_far, near, far, other_near_send, other_far_send, near_send, far_send = outs
    diagonal = [crossed(other_far, "member", "lev"), crossed(other_far_send, "member", "lev", "lon")]
    along_x = [crossed(far, "lev"), crossed(far_send, "lev", "lon")]
    along_y = [crossed(other_near, "member"), crossed(other_near_send, "member", "lon")]
    here = [near, crossed(near_send, "lon")]

    def places(across, swapped):
        return [(across, swapped, other) for other in (False, True)]

    share_of = balanced(balance, places(False, False) + places(True, True), (*here, *diagonal))
    x, y = places(True, False), places(False, True)
    share_of = balanced(balance, [x[0], y[0]], (along_x[0], along_y[0]), share_of)
    return balanced(balance, [x[1], y[1]], (along_x[1], along_y[1]), share_of, True)


def solution(mesh):
    in_specs = (P("lev", "lat", "lon"), P("lev", "lat", "lon"), P(), P("member"), P("member"))
    out_specs = P("member", ("lat", "lev"), "lon")
    return jax.shard_map(
        per_device, mesh=mesh, in_specs=in_specs, out_specs=out_specs, check_vma=False
    )
```

```python
import functools
import math

import jax
import jax.numpy as jnp
from jax import lax
from jax.experimental import pallas as pl
from jax.experimental.pallas import tpu as pltpu
from jax.sharding import PartitionSpec as P

SWEEPS = 12
SOME = 3
noise_scale = math.sqrt(3.0) / 65536.0
LANES, SUB = 128, 8
HALF = LANES // 2
VMEM = pltpu.VMEM
whole = functools.partial(pl.BlockSpec, memory_space=pltpu.VMEM)
scalars = functools.partial(pl.BlockSpec, memory_space=pltpu.SMEM)


def budget(mebibytes):
    return pltpu.CompilerParams(vmem_limit_bytes=mebibytes << 20)


def scramble(values):
    values = values * 1103515245 + 12345
    values = values ^ (values >> 15)
    values = values * 747796405 + 1013904223
    values = values ^ (values >> 13)
    values = values * 277803737
    return values ^ (values >> 16)


def draw(index, stream_base):
    first = scramble(index ^ stream_base)
    second = scramble(first + 1664525)
    total = (
        (first & 65535)
        + ((first >> 16) & 65535)
        + (second & 65535)
        + ((second >> 16) & 65535)
        - 131070
    )
    return total.astype(jnp.float32) * noise_scale


def packed_source(columns, tiles, core):
    lane = columns & (LANES - 1)
    tile = (columns // LANES) + (tiles // 2) * ((lane // HALF) ^ core)
    return (lane & (HALF - 1)) * tiles + tile


def packing(width, tiles, core, axis):
    natural = lax.broadcasted_iota(jnp.int32, (width, width), 1 - axis)
    columns = lax.broadcasted_iota(jnp.int32, (width, width), axis)
    return jnp.where(packed_source(columns, tiles, core) == natural, 1.0, 0.0).astype(jnp.bfloat16)


def split(values):
    high = values.astype(jnp.bfloat16)
    return high, (values - high.astype(jnp.float32)).astype(jnp.bfloat16)


def permuted(values, matrix):
    rows = values.shape[0]
    both = jnp.dot(jnp.concatenate(split(values), axis=0), matrix, preferred_element_type=jnp.float32)
    return both[:rows] + both[rows:]


def edge_rows(some, pairs, halo):
    return -(-some * pairs * halo // SUB) * SUB


def conduct_kernel(halo, some, kept, other, mine, send, mine_edges, send_edges, matrix):
    levels, height, width = kept.shape
    pairs = width // LANES
    matrix[...] = packing(width, 2 * pairs, lax.axis_index("lon"), 1)
    for source, rows, edges in ((other, send, send_edges), (kept, mine, mine_edges)):
        moved = permuted(source[...].reshape(levels * height, width), matrix[...])
        for l in range(levels):
            for v in range(pairs):
                value = moved[l * height : (l + 1) * height, v * LANES : (v + 1) * LANES]
                rows[l, v] = value
                edge = pl.ds((l % some * pairs + v) * halo, halo)
                edges[0, l // some, edge, :] = value[height - halo :]
                edges[1, l // some, edge, :] = value[:halo]


def packed_conduct(halo, kept, other):
    share, height, width = kept.shape
    some, pairs = math.gcd(share, SOME), width // LANES
    rows = jax.ShapeDtypeStruct((share, pairs, height, LANES), jnp.float32)
    edge = jax.ShapeDtypeStruct((2, share // some, edge_rows(some, pairs, halo), LANES), jnp.float32)
    return pl.pallas_call(
        functools.partial(conduct_kernel, halo, some),
        out_shape=(rows, rows, edge, edge),
        in_specs=[whole()] * 2,
        out_specs=(whole(),) * 4,
        scratch_shapes=[VMEM((width, width), jnp.bfloat16)],
        compiler_params=budget(8),
    )(kept, other)


def noise_kernel(levels_here, halo, total_rows, total_cols, base, out):
    levels, tiles, pitch = out.shape[:3]
    quarter = lax.axis_index("member") * 2 + lax.axis_index("lon")
    level0 = lax.axis_index("lev") * levels_here + quarter * levels
    row0 = lax.axis_index("lat") * (total_rows // lax.axis_size("lat")) - halo
    sub = lax.broadcasted_iota(jnp.int32, (SUB, LANES), 0)
    lane = lax.broadcasted_iota(jnp.int32, (SUB, LANES), 1)
    within = sub * (pitch * total_cols) + lane * tiles
    stream = base[...]

    @pl.loop(0, levels)
    def _(l):
        start = ((level0 + l) * total_rows + row0) * total_cols
        for t in range(tiles):
            for k in range(pitch):
                out[l, t, k] = draw(within + (start + k * total_cols + t), stream)


def noise(base, levels_here, halo, shape, total_rows, total_cols):
    return pl.pallas_call(
        functools.partial(noise_kernel, levels_here, halo, total_rows, total_cols),
        out_shape=jax.ShapeDtypeStruct(shape, jnp.float32),
        in_specs=[whole()],
        out_specs=whole(),
        compiler_params=budget(8),
    )(base)


def neighbour_sums(old, tiles, pitch, emit):
    some = range(old.shape[0])

    def row(g, k):
        values = [old[g, t, k] for t in range(tiles)]
        return [pltpu.roll(values[-1], 1, 1), *values, pltpu.roll(values[0], LANES - 1, 1)]

    first = [row(g, 0) for g in some]
    above = [[pltpu.roll(old[g, t, pitch - 1], 1, 0) for t in range(tiles)] for g in some]
    pairs = [[above[g][t] + first[g][t] for t in range(tiles)] for g in some]
    here = first
    for k in range(pitch):
        if k == pitch - 1:
            below = [[None, *(pltpu.roll(v, SUB - 1, 0) for v in first[g][1:-1]), None] for g in some]
        else:
            below = [row(g, k + 1) for g in some]
        for g in some:
            now, later = here[g], below[g]
            fresh = [None if t == 0 and later[0] is None else now[t + 1] + later[t] for t in range(tiles + 1)]
            for t in range(tiles):
                emit(g, t, k, now[t + 1], fresh[t + 1] + pairs[g][t])
            pairs[g] = fresh
        here = below


def diffuse_kernel(halo, halves, start_block, mine, theirs, top, bottom, other_source, own_source, *refs):
    kept, sent = refs[:4], refs[4:8]
    rows, cond, gain, push, inv, u0, u1, res = refs[8:]
    sources = (other_source, own_source)
    tiles, pitch = own_source.shape[1:3]
    pairs, height = mine.shape[1], mine.shape[2]
    final = height // 2
    core = lax.axis_index("lon")
    group = lax.axis_index("lev") if halves else 0
    some = cond.shape[0]

    def on_left(shape):
        lane = lax.broadcasted_iota(jnp.int32, shape, len(shape) - 1)
        return (lane // HALF) == core

    def sweep(old, new):
        def step(g, t, k, value, total):
            new[g, t, k] = push[g, t, k] + gain[g % some, t, k] * total

        neighbour_sums(old, tiles, pitch, step)

    @pl.loop(start_block, start_block + kept[0].shape[0] // some)
    def _(block):
        for g in range(some):
            l = block * some + g
            for v in range(pairs):
                edge = pl.ds((g * pairs + v) * halo, halo)
                for p, q, start in (
                    (top[0, block, edge, :], top[1, block, edge, :], 0),
                    (mine[l, v], theirs[l, v], halo),
                    (bottom[0, block, edge, :], bottom[1, block, edge, :], halo + height),
                ):
                    count = p.shape[0]
                    left = on_left(p.shape)
                    rows[g, v, pl.ds(start, count), :] = jnp.where(left, p, q)
                    rows[g, v + pairs, pl.ds(start, count), :] = pltpu.roll(jnp.where(left, q, p), HALF, 1)
            for t in range(tiles):
                for k in range(pitch):
                    cond[g, t, k] = rows[g, t, pl.ds(k, SUB, stride=pitch), :]

        def prepare(g, t, k, c, total):
            r = 1.0 / (1.0 + c * total)
            q = c * r
            inv[g, t, k] = r
            gain[g, t, k] = q * c
            for i in range(2):
                s = sources[i][block * some + g, t, k]
                push[i * some + g, t, k] = q * s
                u0[i * some + g, t, k] = c * s

        neighbour_sums(cond, tiles, pitch, prepare)

        for i in range(SWEEPS - 1):
            sweep(*((u0, u1) if i % 2 == 0 else (u1, u0)))

        def finish(g, t, k, value, total):
            i, g = divmod(g, some)
            c, s = cond[g, t, k], sources[i][block * some + g, t, k]
            value = jnp.where(c != 0.0, (s + c * total) * inv[g, t, k], 0.0)
            res[i * some + g, t, pl.ds(k, SUB, stride=pitch), :] = value

        neighbour_sums(u1, tiles, pitch, finish)
        left = on_left((height, LANES))
        first = group == 0
        for i in range(2):
            for g in range(some):
                l = (block - start_block) * some + g
                for v in range(pairs):
                    a = res[i * some + g, v, pl.ds(halo, height), :]
                    b = pltpu.roll(res[i * some + g, v + pairs, pl.ds(halo, height), :], HALF, 1)
                    keep, send = jnp.where(left, a, b), jnp.where(left, b, a)
                    for value, close, away in (
                        (keep, kept[2 * i], kept[2 * i + 1]), (send, sent[2 * i], sent[2 * i + 1]),
                    ):
                        upper, lower = value[:final], value[final:]
                        close[l, v] = jnp.where(first, upper, lower)
                        away[l, v] = jnp.where(first, lower, upper)


def diffuse(halo, halves, blocks, *operands):
    levels, pairs, height, _ = operands[0].shape
    tiles, pitch = operands[-1].shape[1:3]
    some = math.gcd(levels, SOME)
    tile = VMEM((some, tiles, pitch, SUB, LANES), jnp.float32)
    both = VMEM((2 * some, tiles, pitch, SUB, LANES), jnp.float32)
    line = VMEM((2 * some, tiles, (pitch + 1) * SUB, LANES), jnp.float32)
    result = jax.ShapeDtypeStruct((len(blocks) * some, pairs, height // 2, LANES), jnp.float32)
    return pl.pallas_call(
        functools.partial(diffuse_kernel, halo, halves, blocks[0]),
        out_shape=(result,) * 8,
        in_specs=[whole()] * len(operands),
        out_specs=(whole(),) * 8,
        scratch_shapes=[line, tile, tile, both, tile, both, both, line],
        compiler_params=budget(18),
    )(*operands)


def unpack(pieces, matrix, out):
    start = 0
    for piece in pieces:
        levels, tiles, height, _ = piece.shape
        values = jnp.concatenate(
            [piece[:, t].reshape(levels * height, LANES) for t in range(tiles)], axis=1
        )
        moved = permuted(values, matrix)
        for t in range(tiles):
            out[start : start + levels, t] = moved[:, t * LANES : (t + 1) * LANES].reshape(levels, height, LANES)
        start += levels


def chosen(balance, places, width):
    total = balance.shape[1]
    core, member, group = (lax.axis_index(a) for a in ("lon", "member", "lev"))
    column = lax.broadcasted_iota(jnp.int32, (total, width), 1)
    level, offset = jnp.full((total, width), -1, jnp.int32), 0
    share = total // 8
    for across, swapped, other in places:
        g = 1 - group if across else group
        m = 1 - member if swapped else member
        first = (g * 4 + m * 2 + (1 - core if other else core)) * share - offset
        level = jnp.where((column >= offset) & (column < offset + share), column + first, level)
        offset += share
    select = jnp.where(lax.broadcasted_iota(jnp.int32, (total, width), 0) == level, 1.0, 0.0).astype(jnp.bfloat16)
    high, low = (
        jnp.dot(v, select, preferred_element_type=jnp.float32).astype(jnp.bfloat16) for v in split(balance[...])
    )
    return jnp.concatenate([high, high, low], axis=1)


def weighted(balance, places, pieces, matrix, columns, emit):
    total = balance.shape[0]
    tiles, height = columns.shape[1:3]
    count, pitch = sum(p.shape[0] for p in pieces), tiles * height
    unpack(pieces, matrix[...], columns)
    flat = columns.reshape(columns.shape[0] * pitch, LANES)
    stacked = chosen(balance, places, count)
    for t in range(tiles):
        for r in range(height):
            top, rest = split(flat[pl.ds(t * height + r, count, stride=pitch), :])
            right = jnp.concatenate([top, rest, top], axis=0)
            value = jnp.dot(stacked, right, preferred_element_type=jnp.float32)
            emit(t, r, pl.ds(t * height + r, total, stride=pitch), value)


def share_kernel(places, weights, *refs):
    *pieces, out, matrix, columns = refs
    earlier = None
    if len(pieces) > len(places):
        earlier, given, *pieces = pieces
        matrix[...] = given[...]
    else:
        tiles = columns.shape[1]
        matrix[...] = packing(tiles * LANES, 2 * tiles, lax.axis_index("lon"), 0)

    def store(t, r, rows, value):
        out[rows, :] = value if earlier is None else earlier[rows, :] + value

    weighted(weights, places, pieces, matrix, columns, store)


def last_kernel(places, weights, earlier, matrix, *refs):
    *pieces, out, columns, result, sent = refs
    total = weights.shape[0]
    tiles, height = columns.shape[1:3]
    copies = []

    def store(t, r, rows, value):
        result[rows, :] = earlier[rows, :] + value
        if r % SUB == SUB - 1:
            some = pl.ds(r - SUB + 1, SUB)
            copy = pltpu.make_async_copy(
                result.reshape(total, tiles, height, LANES).at[:, t, some],
                out.at[:, some, pl.ds(t * LANES, LANES)],
                sent.at[t, r // SUB],
            )
            copy.start()
            copies.append(copy)

    weighted(weights, places, pieces, matrix, columns, store)
    for copy in copies:
        copy.wait()


def balanced(weights, places, pieces, earlier=None, last=False):
    total, count = weights.shape[0], sum(p.shape[0] for p in pieces)
    tiles, height = pieces[0].shape[1:3]
    flat = (total * tiles * height, LANES)
    columns = VMEM((-(-count // SUB) * SUB, tiles, height, LANES), jnp.float32)
    operands = (weights, *(() if earlier is None else earlier), *pieces)
    matrix = jax.ShapeDtypeStruct((tiles * LANES, tiles * LANES), jnp.bfloat16)
    if not last:
        return pl.pallas_call(
            functools.partial(share_kernel, places),
            out_shape=(jax.ShapeDtypeStruct(flat, jnp.float32), matrix),
            in_specs=[whole()] * len(operands),
            out_specs=(whole(), whole()),
            scratch_shapes=[columns],
            compiler_params=budget(10),
        )(*operands)
    return pl.pallas_call(
        functools.partial(last_kernel, places),
        out_shape=jax.ShapeDtypeStruct((total, height, tiles * LANES), jnp.float32),
        in_specs=[whole()] * len(operands),
        out_specs=pl.BlockSpec(memory_space=pl.ANY),
        scratch_shapes=[columns, VMEM(flat, jnp.float32), pltpu.SemaphoreType.DMA((tiles, height // SUB))],
        compiler_params=budget(10),
    )(*operands)


def crossed(block, *axes):
    count = math.prod(lax.axis_size(a) for a in axes)
    return lax.ppermute(block, axes, [(i, count - 1 - i) for i in range(count)])


def shifted(block, step):
    strips = lax.axis_size("lat")
    return lax.ppermute(block, "lat", [(i, i + step) for i in range(strips) if 0 <= i + step < strips])


def part(block, index, size, axis):
    return lax.dynamic_slice_in_dim(block, index * size, size, axis=axis)


def gathered(kept, came, balance, levels):
    core, member, groups = (lax.axis_index("lon"), lax.axis_index("member"), lax.axis_size("lev"))
    halves = [jnp.concatenate([*half], axis=2) for half in (kept[2:], came[2:], kept[:2], came[:2])]
    rows = jnp.concatenate([jnp.stack(halves[:2]), crossed(jnp.stack(halves[2:]), "member")])
    pieces = lax.all_to_all(rows, "lev", split_axis=3, concat_axis=0, tiled=True)
    count, share, tiles, height, _ = pieces.shape
    values = pieces.transpose(0, 1, 3, 2, 4).reshape(count * share, height, tiles * LANES)
    matrix = packing(tiles * LANES, 2 * tiles, core, 0).astype(jnp.float32)
    values = jnp.einsum("mrp,pc->mrc", values, matrix, precision=lax.Precision.HIGHEST)
    spare = 4 * share - levels
    padded = jnp.pad(balance.reshape(-1, groups, levels), ((0, 0), (0, 0), (0, spare)))
    padded = padded.reshape(-1, groups * 4 * share)
    order = [(g, m, c) for g in range(groups) for m in (member, 1 - member) for c in (core, 1 - core)]
    weights = jnp.concatenate([part(padded, g * 4 + m * 2 + c, share, 1) for g, m, c in order], axis=1)
    return jnp.einsum("lm,mrc->lrc", weights, values, precision=lax.Precision.HIGHEST)


def per_device(land_mask, diffusivity, balance, member_id, counter_key):
    levels, height, breadth = land_mask.shape
    members, cores, groups, strips = (lax.axis_size(a) for a in ("member", "lon", "lev", "lat"))
    core, member, group = (lax.axis_index(a) for a in ("lon", "member", "lev"))
    assert members == 2 and cores == 2 and height > SWEEPS
    halo = SWEEPS
    pitch = (height + 2 * halo) // SUB
    share = -(-levels // 4)
    spare = share * 4 - levels
    if spare:
        land_mask, diffusivity = (jnp.pad(v, ((0, spare), (0, 0), (0, 0))) for v in (land_mask, diffusivity))
    kept, other = (
        part(diffusivity, member * 2 + c, share, 0) * part(land_mask, member * 2 + c, share, 0).astype(jnp.float32)
        for c in (core, 1 - core)
    )
    mine, send, mine_edges, send_edges = packed_conduct(halo, kept, other)
    edges = jnp.stack([mine_edges, crossed(send_edges, "lon")], axis=1)
    theirs = crossed(send, "lon")
    top, bottom = shifted(edges[0], 1), shifted(edges[1], -1)
    base = jnp.broadcast_to(counter_key[0] * 69069 + member_id[0] * 362437, (SUB, LANES))
    other_base = crossed(base, "member")
    tiles = breadth * cores // LANES
    sizes = (levels, halo, (share, tiles, pitch, SUB, LANES), height * strips, breadth * cores)
    own_source = noise(base, *sizes)
    other_source = noise(other_base, *sizes)
    blocks = range(share // math.gcd(share, SOME))
    operands = (mine, theirs, top, bottom, other_source, own_source)

    if groups != 2:
        outs = diffuse(halo, False, blocks, *operands)
        return gathered(outs[:4], crossed(jnp.stack(outs[4:]), "lon"), balance, levels)
    outs = diffuse(halo, True, blocks, *operands)
    other_near, other_far, near, far, other_near_send, other_far_send, near_send, far_send = outs
    diagonal = [crossed(other_far, "member", "lev"), crossed(other_far_send, "member", "lev", "lon")]
    along_x = [crossed(far, "lev"), crossed(far_send, "lev", "lon")]
    along_y = [crossed(other_near, "member"), crossed(other_near_send, "member", "lon")]
    here = [near, crossed(near_send, "lon")]

    def places(across, swapped):
        return [(across, swapped, other) for other in (False, True)]

    share_of = balanced(balance, places(False, False) + places(True, True), (*here, *diagonal))
    x, y = places(True, False), places(False, True)
    share_of = balanced(balance, [x[0], y[0]], (along_x[0], along_y[0]), share_of)
    return balanced(balance, [x[1], y[1]], (along_x[1], along_y[1]), share_of, True)


def solution(mesh):
    in_specs = (P("lev", "lat", "lon"), P("lev", "lat", "lon"), P(), P("member"), P("member"))
    out_specs = P("member", ("lat", "lev"), "lon")
    return jax.shard_map(
        per_device, mesh=mesh, in_specs=in_specs, out_specs=out_specs, check_vma=False
    )
```

```python
import functools
import math

import jax
import jax.numpy as jnp
from jax import lax
from jax.experimental import pallas as pl
from jax.experimental.pallas import tpu as pltpu
from jax.sharding import PartitionSpec as P

SWEEPS = 12
SOME = 3
noise_scale = math.sqrt(3.0) / 65536.0
LANES, SUB = 128, 8
HALF = LANES // 2
VMEM = pltpu.VMEM
whole = functools.partial(pl.BlockSpec, memory_space=pltpu.VMEM)
scalars = functools.partial(pl.BlockSpec, memory_space=pltpu.SMEM)


def budget(mebibytes):
    return pltpu.CompilerParams(vmem_limit_bytes=mebibytes << 20)


def scramble(values):
    values = values * 1103515245 + 12345
    values = values ^ (values >> 15)
    values = values * 747796405 + 1013904223
    values = values ^ (values >> 13)
    values = values * 277803737
    return values ^ (values >> 16)


def draw(index, stream_base):
    first = scramble(index ^ stream_base)
    second = scramble(first + 1664525)
    total = (
        (first & 65535)
        + ((first >> 16) & 65535)
        + (second & 65535)
        + ((second >> 16) & 65535)
        - 131070
    )
    return total.astype(jnp.float32) * noise_scale


def packed_source(columns, tiles, core):
    lane = columns & (LANES - 1)
    tile = (columns // LANES) + (tiles // 2) * ((lane // HALF) ^ core)
    return (lane & (HALF - 1)) * tiles + tile


def packing(width, tiles, core, axis):
    natural = lax.broadcasted_iota(jnp.int32, (width, width), 1 - axis)
    columns = lax.broadcasted_iota(jnp.int32, (width, width), axis)
    return jnp.where(packed_source(columns, tiles, core) == natural, 1.0, 0.0).astype(jnp.bfloat16)


def split(values):
    high = values.astype(jnp.bfloat16)
    return high, (values - high.astype(jnp.float32)).astype(jnp.bfloat16)


def permuted(values, matrix):
    rows = values.shape[0]
    both = jnp.dot(jnp.concatenate(split(values), axis=0), matrix, preferred_element_type=jnp.float32)
    return both[:rows] + both[rows:]


def edge_rows(some, pairs, halo):
    return -(-some * pairs * halo // SUB) * SUB


def conduct_kernel(halo, some, kept, other, mine, send, mine_edges, send_edges, matrix):
    levels, height, width = kept.shape
    pairs = width // LANES
    matrix[...] = packing(width, 2 * pairs, lax.axis_index("lon"), 1)
    for source, rows, edges in ((other, send, send_edges), (kept, mine, mine_edges)):
        moved = permuted(source[...].reshape(levels * height, width), matrix[...])
        for l in range(levels):
            for v in range(pairs):
                value = moved[l * height : (l + 1) * height, v * LANES : (v + 1) * LANES]
                rows[l, v] = value
                edge = pl.ds((l % some * pairs + v) * halo, halo)
                edges[0, l // some, edge, :] = value[height - halo :]
                edges[1, l // some, edge, :] = value[:halo]


def packed_conduct(halo, kept, other):
    share, height, width = kept.shape
    some, pairs = math.gcd(share, SOME), width // LANES
    rows = jax.ShapeDtypeStruct((share, pairs, height, LANES), jnp.float32)
    edge = jax.ShapeDtypeStruct((2, share // some, edge_rows(some, pairs, halo), LANES), jnp.float32)
    return pl.pallas_call(
        functools.partial(conduct_kernel, halo, some),
        out_shape=(rows, rows, edge, edge),
        in_specs=[whole()] * 2,
        out_specs=(whole(),) * 4,
        scratch_shapes=[VMEM((width, width), jnp.bfloat16)],
        compiler_params=budget(8),
    )(kept, other)


def noise_kernel(levels_here, halo, total_rows, total_cols, base, out):
    levels, tiles, pitch = out.shape[:3]
    quarter = lax.axis_index("member") * 2 + lax.axis_index("lon")
    level0 = lax.axis_index("lev") * levels_here + quarter * levels
    row0 = lax.axis_index("lat") * (total_rows // lax.axis_size("lat")) - halo
    sub = lax.broadcasted_iota(jnp.int32, (SUB, LANES), 0)
    lane = lax.broadcasted_iota(jnp.int32, (SUB, LANES), 1)
    within = sub * (pitch * total_cols) + lane * tiles
    stream = base[...]

    @pl.loop(0, levels)
    def _(l):
        start = ((level0 + l) * total_rows + row0) * total_cols
        for t in range(tiles):
            for k in range(pitch):
                out[l, t, k] = draw(within + (start + k * total_cols + t), stream)


def noise(base, levels_here, halo, shape, total_rows, total_cols):
    return pl.pallas_call(
        functools.partial(noise_kernel, levels_here, halo, total_rows, total_cols),
        out_shape=jax.ShapeDtypeStruct(shape, jnp.float32),
        in_specs=[whole()],
        out_specs=whole(),
        compiler_params=budget(8),
    )(base)


def neighbour_sums(old, tiles, pitch, emit):
    some = range(old.shape[0])

    def row(g, k):
        values = [old[g, t, k] for t in range(tiles)]
        return [pltpu.roll(values[-1], 1, 1), *values, pltpu.roll(values[0], LANES - 1, 1)]

    first = [row(g, 0) for g in some]
    above = [[pltpu.roll(old[g, t, pitch - 1], 1, 0) for t in range(tiles)] for g in some]
    pairs = [[above[g][t] + first[g][t] for t in range(tiles)] for g in some]
    here = first
    for k in range(pitch):
        if k == pitch - 1:
            below = [[None, *(pltpu.roll(v, SUB - 1, 0) for v in first[g][1:-1]), None] for g in some]
        else:
            below = [row(g, k + 1) for g in some]
        for g in some:
            now, later = here[g], below[g]
            fresh = [None if t == 0 and later[0] is None else now[t + 1] + later[t] for t in range(tiles + 1)]
            for t in range(tiles):
                emit(g, t, k, now[t + 1], fresh[t + 1] + pairs[g][t])
            pairs[g] = fresh
        here = below


def diffuse_kernel(halo, halves, start_block, mine, theirs, top, bottom, other_source, own_source, *refs):
    kept, sent = refs[:4], refs[4:8]
    rows, cond, gain, push, inv, u0, u1, res = refs[8:]
    sources = (other_source, own_source)
    tiles, pitch = own_source.shape[1:3]
    pairs, height = mine.shape[1], mine.shape[2]
    final = height // 2
    core = lax.axis_index("lon")
    group = lax.axis_index("lev") if halves else 0
    some = cond.shape[0]

    def on_left(shape):
        lane = lax.broadcasted_iota(jnp.int32, shape, len(shape) - 1)
        return (lane // HALF) == core

    def sweep(old, new):
        def step(g, t, k, value, total):
            new[g, t, k] = push[g, t, k] + gain[g % some, t, k] * total

        neighbour_sums(old, tiles, pitch, step)

    @pl.loop(start_block, start_block + kept[0].shape[0] // some)
    def _(block):
        for g in range(some):
            l = block * some + g
            for v in range(pairs):
                edge = pl.ds((g * pairs + v) * halo, halo)
                for p, q, start in (
                    (top[0, block, edge, :], top[1, block, edge, :], 0),
                    (mine[l, v], theirs[l, v], halo),
                    (bottom[0, block, edge, :], bottom[1, block, edge, :], halo + height),
                ):
                    count = p.shape[0]
                    left = on_left(p.shape)
                    rows[g, v, pl.ds(start, count), :] = jnp.where(left, p, q)
                    rows[g, v + pairs, pl.ds(start, count), :] = pltpu.roll(jnp.where(left, q, p), HALF, 1)
            for t in range(tiles):
                for k in range(pitch):
                    cond[g, t, k] = rows[g, t, pl.ds(k, SUB, stride=pitch), :]

        def prepare(g, t, k, c, total):
            r = 1.0 / (1.0 + c * total)
            q = c * r
            inv[g, t, k] = r
            gain[g, t, k] = q * c
            for i in range(2):
                s = sources[i][block * some + g, t, k]
                push[i * some + g, t, k] = q * s
                u0[i * some + g, t, k] = c * s

        neighbour_sums(cond, tiles, pitch, prepare)

        for i in range(SWEEPS - 1):
            sweep(*((u0, u1) if i % 2 == 0 else (u1, u0)))

        def finish(g, t, k, value, total):
            i, g = divmod(g, some)
            c, s = cond[g, t, k], sources[i][block * some + g, t, k]
            value = jnp.where(c != 0.0, (s + c * total) * inv[g, t, k], 0.0)
            res[i * some + g, t, pl.ds(k, SUB, stride=pitch), :] = value

        neighbour_sums(u1, tiles, pitch, finish)
        left = on_left((height, LANES))
        first = group == 0
        for i in range(2):
            for g in range(some):
                l = (block - start_block) * some + g
                for v in range(pairs):
                    a = res[i * some + g, v, pl.ds(halo, height), :]
                    b = pltpu.roll(res[i * some + g, v + pairs, pl.ds(halo, height), :], HALF, 1)
                    keep, send = jnp.where(left, a, b), jnp.where(left, b, a)
                    for value, close, away in (
                        (keep, kept[2 * i], kept[2 * i + 1]), (send, sent[2 * i], sent[2 * i + 1]),
                    ):
                        upper, lower = value[:final], value[final:]
                        close[l, v] = jnp.where(first, upper, lower)
                        away[l, v] = jnp.where(first, lower, upper)


def diffuse(halo, halves, blocks, *operands):
    levels, pairs, height, _ = operands[0].shape
    tiles, pitch = operands[-1].shape[1:3]
    some = math.gcd(levels, SOME)
    tile = VMEM((some, tiles, pitch, SUB, LANES), jnp.float32)
    both = VMEM((2 * some, tiles, pitch, SUB, LANES), jnp.float32)
    line = VMEM((2 * some, tiles, (pitch + 1) * SUB, LANES), jnp.float32)
    result = jax.ShapeDtypeStruct((len(blocks) * some, pairs, height // 2, LANES), jnp.float32)
    return pl.pallas_call(
        functools.partial(diffuse_kernel, halo, halves, blocks[0]),
        out_shape=(result,) * 8,
        in_specs=[whole()] * len(operands),
        out_specs=(whole(),) * 8,
        scratch_shapes=[line, tile, tile, both, tile, both, both, line],
        compiler_params=budget(18),
    )(*operands)


def unpack(pieces, matrix, out):
    levels, tiles, height, _ = pieces[0].shape
    values = [
        jnp.concatenate([piece[:, t].reshape(levels * height, LANES) for t in range(tiles)], axis=1)
        for piece in pieces
    ]
    moved = permuted(jnp.concatenate(values, axis=0), matrix)
    count = levels * len(pieces)
    for t in range(tiles):
        out[:count, t] = moved[:, t * LANES : (t + 1) * LANES].reshape(count, height, LANES)


def chosen(balance, places, width):
    total = balance.shape[1]
    core, member, group = (lax.axis_index(a) for a in ("lon", "member", "lev"))
    column = lax.broadcasted_iota(jnp.int32, (total, width), 1)
    level, offset = jnp.full((total, width), -1, jnp.int32), 0
    share = total // 8
    for across, swapped, other in places:
        g = 1 - group if across else group
        m = 1 - member if swapped else member
        first = (g * 4 + m * 2 + (1 - core if other else core)) * share - offset
        level = jnp.where((column >= offset) & (column < offset + share), column + first, level)
        offset += share
    select = jnp.where(lax.broadcasted_iota(jnp.int32, (total, width), 0) == level, 1.0, 0.0).astype(jnp.bfloat16)
    high, low = (
        jnp.dot(v, select, preferred_element_type=jnp.float32).astype(jnp.bfloat16) for v in split(balance[...])
    )
    return jnp.concatenate([high, high, low], axis=1)


def weighted(balance, places, pieces, matrix, columns, emit):
    total = balance.shape[0]
    tiles, height = columns.shape[1:3]
    count, pitch = sum(p.shape[0] for p in pieces), tiles * height
    unpack(pieces, matrix[...], columns)
    flat = columns.reshape(columns.shape[0] * pitch, LANES)
    stacked = chosen(balance, places, count)
    for t in range(tiles):
        for r in range(height):
            top, rest = split(flat[pl.ds(t * height + r, count, stride=pitch), :])
            right = jnp.concatenate([top, rest, top], axis=0)
            value = jnp.dot(stacked, right, preferred_element_type=jnp.float32)
            emit(t, r, pl.ds(t * height + r, total, stride=pitch), value)


def share_kernel(places, weights, *refs):
    *pieces, out, matrix, columns = refs
    earlier = None
    if len(pieces) > len(places):
        earlier, given, *pieces = pieces
        matrix[...] = given[...]
    else:
        tiles = columns.shape[1]
        matrix[...] = packing(tiles * LANES, 2 * tiles, lax.axis_index("lon"), 0)

    def store(t, r, rows, value):
        out[rows, :] = value if earlier is None else earlier[rows, :] + value

    weighted(weights, places, pieces, matrix, columns, store)


def last_kernel(places, weights, earlier, matrix, *refs):
    *pieces, out, columns, result, sent = refs
    total = weights.shape[0]
    tiles, height = columns.shape[1:3]
    copies = []

    def store(t, r, rows, value):
        result[rows, :] = earlier[rows, :] + value
        if r % SUB == SUB - 1:
            some = pl.ds(r - SUB + 1, SUB)
            copy = pltpu.make_async_copy(
                result.reshape(total, tiles, height, LANES).at[:, t, some],
                out.at[:, some, pl.ds(t * LANES, LANES)],
                sent.at[t, r // SUB],
            )
            copy.start()
            copies.append(copy)

    weighted(weights, places, pieces, matrix, columns, store)
    for copy in copies:
        copy.wait()


def balanced(weights, places, pieces, earlier=None, last=False):
    total, count = weights.shape[0], sum(p.shape[0] for p in pieces)
    tiles, height = pieces[0].shape[1:3]
    flat = (total * tiles * height, LANES)
    columns = VMEM((-(-count // SUB) * SUB, tiles, height, LANES), jnp.float32)
    operands = (weights, *(() if earlier is None else earlier), *pieces)
    matrix = jax.ShapeDtypeStruct((tiles * LANES, tiles * LANES), jnp.bfloat16)
    if not last:
        return pl.pallas_call(
            functools.partial(share_kernel, places),
            out_shape=(jax.ShapeDtypeStruct(flat, jnp.float32), matrix),
            in_specs=[whole()] * len(operands),
            out_specs=(whole(), whole()),
            scratch_shapes=[columns],
            compiler_params=budget(10),
        )(*operands)
    return pl.pallas_call(
        functools.partial(last_kernel, places),
        out_shape=jax.ShapeDtypeStruct((total, height, tiles * LANES), jnp.float32),
        in_specs=[whole()] * len(operands),
        out_specs=pl.BlockSpec(memory_space=pl.ANY),
        scratch_shapes=[columns, VMEM(flat, jnp.float32), pltpu.SemaphoreType.DMA((tiles, height // SUB))],
        compiler_params=budget(10),
    )(*operands)


def crossed(block, *axes):
    count = math.prod(lax.axis_size(a) for a in axes)
    return lax.ppermute(block, axes, [(i, count - 1 - i) for i in range(count)])


def shifted(block, step):
    strips = lax.axis_size("lat")
    return lax.ppermute(block, "lat", [(i, i + step) for i in range(strips) if 0 <= i + step < strips])


def part(block, index, size, axis):
    return lax.dynamic_slice_in_dim(block, index * size, size, axis=axis)


def gathered(kept, came, balance, levels):
    core, member, groups = (lax.axis_index("lon"), lax.axis_index("member"), lax.axis_size("lev"))
    halves = [jnp.concatenate([*half], axis=2) for half in (kept[2:], came[2:], kept[:2], came[:2])]
    rows = jnp.concatenate([jnp.stack(halves[:2]), crossed(jnp.stack(halves[2:]), "member")])
    pieces = lax.all_to_all(rows, "lev", split_axis=3, concat_axis=0, tiled=True)
    count, share, tiles, height, _ = pieces.shape
    values = pieces.transpose(0, 1, 3, 2, 4).reshape(count * share, height, tiles * LANES)
    matrix = packing(tiles * LANES, 2 * tiles, core, 0).astype(jnp.float32)
    values = jnp.einsum("mrp,pc->mrc", values, matrix, precision=lax.Precision.HIGHEST)
    spare = 4 * share - levels
    padded = jnp.pad(balance.reshape(-1, groups, levels), ((0, 0), (0, 0), (0, spare)))
    padded = padded.reshape(-1, groups * 4 * share)
    order = [(g, m, c) for g in range(groups) for m in (member, 1 - member) for c in (core, 1 - core)]
    weights = jnp.concatenate([part(padded, g * 4 + m * 2 + c, share, 1) for g, m, c in order], axis=1)
    return jnp.einsum("lm,mrc->lrc", weights, values, precision=lax.Precision.HIGHEST)


def per_device(land_mask, diffusivity, balance, member_id, counter_key):
    levels, height, breadth = land_mask.shape
    members, cores, groups, strips = (lax.axis_size(a) for a in ("member", "lon", "lev", "lat"))
    core, member, group = (lax.axis_index(a) for a in ("lon", "member", "lev"))
    assert members == 2 and cores == 2 and height > SWEEPS
    halo = SWEEPS
    pitch = (height + 2 * halo) // SUB
    share = -(-levels // 4)
    spare = share * 4 - levels
    if spare:
        land_mask, diffusivity = (jnp.pad(v, ((0, spare), (0, 0), (0, 0))) for v in (land_mask, diffusivity))
    kept, other = (
        part(diffusivity, member * 2 + c, share, 0) * part(land_mask, member * 2 + c, share, 0).astype(jnp.float32)
        for c in (core, 1 - core)
    )
    mine, send, mine_edges, send_edges = packed_conduct(halo, kept, other)
    edges = jnp.stack([mine_edges, crossed(send_edges, "lon")], axis=1)
    theirs = crossed(send, "lon")
    top, bottom = shifted(edges[0], 1), shifted(edges[1], -1)
    base = jnp.broadcast_to(counter_key[0] * 69069 + member_id[0] * 362437, (SUB, LANES))
    other_base = crossed(base, "member")
    tiles = breadth * cores // LANES
    sizes = (levels, halo, (share, tiles, pitch, SUB, LANES), height * strips, breadth * cores)
    own_source = noise(base, *sizes)
    other_source = noise(other_base, *sizes)
    blocks = range(share // math.gcd(share, SOME))
    operands = (mine, theirs, top, bottom, other_source, own_source)

    if groups != 2:
        outs = diffuse(halo, False, blocks, *operands)
        return gathered(outs[:4], crossed(jnp.stack(outs[4:]), "lon"), balance, levels)
    outs = diffuse(halo, True, blocks, *operands)
    other_near, other_far, near, far, other_near_send, other_far_send, near_send, far_send = outs
    diagonal = [crossed(other_far, "member", "lev"), crossed(other_far_send, "member", "lev", "lon")]
    along_x = [crossed(far, "lev"), crossed(far_send, "lev", "lon")]
    along_y = [crossed(other_near, "member"), crossed(other_near_send, "member", "lon")]
    here = [near, crossed(near_send, "lon")]

    def places(across, swapped):
        return [(across, swapped, other) for other in (False, True)]

    share_of = balanced(balance, places(False, False) + places(True, True), (*here, *diagonal))
    x, y = places(True, False), places(False, True)
    share_of = balanced(balance, [x[0], y[0]], (along_x[0], along_y[0]), share_of)
    return balanced(balance, [x[1], y[1]], (along_x[1], along_y[1]), share_of, True)


def solution(mesh):
    in_specs = (P("lev", "lat", "lon"), P("lev", "lat", "lon"), P(), P("member"), P("member"))
    out_specs = P("member", ("lat", "lev"), "lon")
    return jax.shard_map(
        per_device, mesh=mesh, in_specs=in_specs, out_specs=out_specs, check_vma=False
    )
```
